1024 devices in a mesh: dx: 8 (over y), dy: 8 (over z), dz: 16 (over x, core).
Axes of the slice: x: 8, y: 8, z: 8, core: 2. Of those that a mesh axis runs over, the one named last changes fastest.
Arguments:
- gas_core: float32 [5, 8, 8, 131072], P(None, 'dx', 'dy', 'dz')
- gas_vel: float32 [3, 8, 8, 131072], P(None, 'dx', 'dy', 'dz'), may hold values from -6 to 6
- gas_energy: float32 [8, 8, 131072], P('dx', 'dy', 'dz'), may hold values from 0.5 to 2
- cell_pairs: int32 [2, 8, 8, 256], P(None, 'dx', 'dy', 'dz'), may hold values from 0 to 35, as said below
- bh_coord: float32 [3, 8, 8, 2048], P(None, 'dx', 'dy', 'dz')
- bh_vel: float32 [3, 8, 8, 2048], P(None, 'dx', 'dy', 'dz'), may hold values from -6 to 6
- bh_mass: float32 [8, 8, 2048], P('dx', 'dy', 'dz'), may hold values from 20 to 80
- bh_soft: float32 [8, 8, 2048], P('dx', 'dy', 'dz'), may hold values from 8 to 32
- mem_gas: int32 [8, 8, 49152], P('dx', 'dy', 'dz'), may hold values from 0 to 8191
- mem_slot: int32 [8, 8, 49152], P('dx', 'dy', 'dz'), may hold values from 0 to 127, as said below
- send_count: int32 [8, 8, 2048], P('dx', 'dy', 'dz'), may hold values from 0 to 24, as said below
Outputs:
- density: float32 [8, 8, 131072], P('dx', 'dy', 'dz')
- gas_update: float32 [2, 8, 8, 131072], P(None, 'dx', 'dy', 'dz')
- bh_update: float32 [2, 8, 8, 2048], P(None, 'dx', 'dy', 'dz')
The draws below stay inside these ranges and needn't reach their ends.
Inputs may be any that keep to these rules, and one draw needn't show every extreme that they name: `cell_pairs`: row 0 is a cell of the device and row 1 an extended cell at most 10 cells from it and never the same cell; the pairs of one device are distinct; every device lists (0, 9) and (15, 26). `mem_gas`: A particle may appear in several entries. `mem_slot`: the live entries of a block are ordered by slot; all live entries of one black hole come from a single device of its slab, whose domain holds the black hole, and they number 24 // 2 to 24. `send_count`: in every dx slab some blocks hold 24 live entries.
All inputs are finite; a program needn't handle non-finite values.
Results may differ from the reference program's by a relative error of at most 0.0003.
Values sent between devices are 32-bit elements; how exact they have to be, the bound alone decides.
No kernel may reach another device: no remote copies, remote signals or barrier semaphores. Data moves between devices by JAX's collectives and lax.ppermute only.
A program may use at most 64 MiB of HBM per device.

```python
import math
import jax
import jax.numpy as jnp
from jax import lax

CELL = 512
CPD = 16
BND = 10
NPAIR = 16
CAP = 24
NB = 128
NZ_ALL = 131072
BZ_ALL = 2048
ENTRY_ALL = 49152
N_DX = 8
N_DY = 8
N_DZ = 16


face_width = 32.0


cell_height = 0.5


def draw_gas_core(key, part):
    keys = jax.random.split(key, 5)
    shape = (N_DX, N_DY, N_DZ, CPD, CELL)
    slab = jnp.arange(N_DX, dtype=jnp.float32).reshape(N_DX, 1, 1, 1, 1)
    column = jnp.arange(N_DY, dtype=jnp.float32).reshape(1, N_DY, 1, 1, 1)
    layer = jnp.arange(N_DZ, dtype=jnp.float32).reshape(1, 1, N_DZ, 1, 1)
    cell_index = jnp.arange(CPD, dtype=jnp.float32).reshape(1, 1, 1, CPD, 1)
    pos_x = face_width * (slab + jax.random.uniform(keys[0], shape, jnp.float32))
    pos_y = face_width * (column + jax.random.uniform(keys[1], shape, jnp.float32))
    pos_z = cell_height * (CPD * layer + cell_index + jax.random.uniform(keys[2], shape, jnp.float32))
    mass = jnp.exp(jax.random.uniform(keys[3], shape, jnp.float32, math.log(0.5), math.log(2.0)))
    smooth = jnp.exp(jax.random.uniform(keys[4], shape, jnp.float32, math.log(2.5), math.log(6.0)))
    stacked = jnp.stack([pos_x, pos_y, pos_z, mass, smooth])
    return stacked.reshape(5, N_DX, N_DY, N_DZ * CPD * CELL).astype(jnp.float32)


def kernel_plan(key):
    group = N_DY * N_DZ
    base = jax.random.fold_in(key, 11)
    first, second, third = jax.random.split(base, 3)

    def slab_offsets(sub):
        return jax.random.permutation(sub, group).astype(jnp.int32)
    offsets = jax.vmap(slab_offsets)(jax.random.split(first, N_DX))
    counts = jax.random.randint(second, (N_DX, group, NB), CAP // 2, CAP + 1).astype(jnp.int32)
    slot_ids = jnp.arange(NB, dtype=jnp.int32).reshape(1, 1, NB)
    counts = jnp.where((slot_ids == 1) | (slot_ids == 2), CAP, counts)
    return (offsets, counts, third)


def entry_plan(key):
    group = N_DY * N_DZ
    offsets, counts, third = kernel_plan(key)
    sender = jnp.arange(group, dtype=jnp.int32).reshape(1, group, 1, 1)
    owner = jnp.arange(group, dtype=jnp.int32).reshape(1, 1, group, 1)
    host = (owner + offsets.reshape(N_DX, 1, 1, NB)) % group
    width = jnp.where(host == sender, counts.reshape(N_DX, 1, group, NB), 0)
    cum = jnp.cumsum(width, axis=3).astype(jnp.int32)
    total = cum[..., NB - 1]
    position = jnp.arange(CAP, dtype=jnp.int32).reshape(1, 1, 1, CAP)
    slot = jnp.sum((cum[:, :, :, None, :] <= position[..., None]).astype(jnp.int32), axis=4)
    filler = jax.random.randint(third, (N_DX, group, group, CAP), 0, NB).astype(jnp.int32)
    slot = jnp.where(position < total[..., None], slot, filler)
    return (slot, total)


def draw_bh_coord(key, part):
    group = N_DY * N_DZ
    offsets, counts, third = kernel_plan(key)
    keys = jax.random.split(jax.random.fold_in(key, 23), 3)
    owner = jnp.arange(group, dtype=jnp.int32).reshape(1, group, 1)
    host = (owner + offsets.reshape(N_DX, 1, NB)) % group
    host_y = (host // N_DZ).astype(jnp.float32)
    host_z = (host % N_DZ).astype(jnp.float32)
    shape = (N_DX, group, NB)
    slab = jnp.arange(N_DX, dtype=jnp.float32).reshape(N_DX, 1, 1)
    pos_x = face_width * (slab + jax.random.uniform(keys[0], shape, jnp.float32))
    pos_y = face_width * (host_y + jax.random.uniform(keys[1], shape, jnp.float32))
    pos_z = cell_height * CPD * (host_z + jax.random.uniform(keys[2], shape, jnp.float32))
    return jnp.stack([pos_x, pos_y, pos_z]).reshape(3, N_DX, N_DY, N_DZ * NB).astype(jnp.float32)


def draw_cell_pairs(key, part):
    devices_all = N_DX * N_DY * N_DZ
    span = 2 * BND
    candidates = CPD * span
    forced_low = BND - 1
    forced_high = (CPD - 1) * span + BND

    def one_device(sub):
        first, second = jax.random.split(sub)
        picks = jax.random.permutation(first, candidates - 2)[:NPAIR - 2].astype(jnp.int32)
        picks = picks + (picks >= forced_low).astype(jnp.int32)
        picks = picks + (picks >= forced_high).astype(jnp.int32)
        every = jnp.concatenate([jnp.array([forced_low, forced_high], dtype=jnp.int32), picks])
        every = jax.random.permutation(second, every)
        home = every // span
        rest = every % span
        offset = rest - BND + (rest >= BND).astype(jnp.int32)
        return jnp.stack([home, home + BND + offset])
    listed = jax.vmap(one_device)(jax.random.split(jax.random.fold_in(key, 7), devices_all))
    return jnp.moveaxis(listed, 0, 1).reshape(2, N_DX, N_DY, N_DZ * NPAIR).astype(jnp.int32)


def draw_send_count(key, part):
    group = N_DY * N_DZ
    slot, total = entry_plan(key)
    return total.reshape(N_DX, N_DY, N_DZ * group).astype(jnp.int32)


def draw_mem_slot(key, part):
    group = N_DY * N_DZ
    slot, total = entry_plan(key)
    return slot.reshape(N_DX, N_DY, N_DZ * group * CAP).astype(jnp.int32)


def touch_ends(values, stream_key, low, high):
    spot = [jax.random.randint(jax.random.fold_in(stream_key, axis), (), 0, length) for axis, length in enumerate(values.shape)]
    main_axis = values.shape.index(max(values.shape))
    beside = spot[:main_axis] + [(spot[main_axis] + 1) % values.shape[main_axis]] + spot[main_axis + 1:]
    return values.at[tuple(spot)].set(low).at[tuple(beside)].set(high)


def shard_levels(stream_key, dims, cuts, least, top_value):
    level, own = 1.0, jax.random.fold_in(stream_key, 6)
    for axis_at, shards_of in cuts:
        heights = jnp.exp(jax.random.uniform(jax.random.fold_in(own, axis_at), (shards_of,), jnp.float32, least / len(cuts), top_value / len(cuts)))
        level = level * jnp.repeat(heights, dims[axis_at] // shards_of).reshape([-1 if axis == axis_at else 1 for axis in range(len(dims))])
    return level


def centred(rng, extent, spread, most, cuts=(), held_as=jnp.bfloat16):
    values = spread * jax.random.normal(rng, extent, jnp.float32)
    if cuts:
        values = values * shard_levels(rng, extent, cuts, -0.22, 0.18)
    return jnp.clip(values, -most, most).astype(held_as)


def setup_inputs(seed: int = 0) -> dict:
    key_of = jax.random.split(jax.random.key(seed), 12)
    return {
        "gas_core": draw_gas_core(jax.random.fold_in(key_of[11], 71), 0),
        "gas_vel": centred(key_of[1], (3, N_DX, N_DY, NZ_ALL), 1.0, 6.0, ((1, 8), (2, 8), (3, 16)), jnp.float32),
        "gas_energy": jnp.clip(jnp.exp(math.log(2.0) - 1.3862944 * jax.random.uniform(key_of[2], (N_DX, N_DY, NZ_ALL), jnp.float32) ** shard_levels(key_of[2], (N_DX, N_DY, NZ_ALL), ((0, 8), (1, 8), (2, 16)), -0.2, 0.2)), 0.5, 2.0),
        "cell_pairs": draw_cell_pairs(jax.random.fold_in(key_of[11], 71), 0),
        "bh_coord": draw_bh_coord(jax.random.fold_in(key_of[11], 71), 0),
        "bh_vel": centred(key_of[5], (3, N_DX, N_DY, BZ_ALL), 1.0, 6.0, ((1, 8), (2, 8), (3, 16)), jnp.float32),
        "bh_mass": jnp.clip(jnp.exp(math.log(80.0) - 1.3862944 * jax.random.uniform(key_of[6], (N_DX, N_DY, BZ_ALL), jnp.float32) ** shard_levels(key_of[6], (N_DX, N_DY, BZ_ALL), ((0, 8), (1, 8), (2, 16)), -0.2, 0.2)), 20.0, 80.0),
        "bh_soft": jnp.clip(jnp.exp(math.log(32.0) - 1.3862944 * jax.random.uniform(key_of[7], (N_DX, N_DY, BZ_ALL), jnp.float32) ** shard_levels(key_of[7], (N_DX, N_DY, BZ_ALL), ((0, 8), (1, 8), (2, 16)), -0.2, 0.2)), 8.0, 32.0),
        "mem_gas": touch_ends(jax.random.randint(key_of[8], (N_DX, N_DY, ENTRY_ALL), 0, CPD * CELL), jax.random.fold_in(key_of[8], 1), 0, (CPD * CELL) - 1).astype(jnp.int32),
        "mem_slot": draw_mem_slot(jax.random.fold_in(key_of[11], 71), 0),
        "send_count": draw_send_count(jax.random.fold_in(key_of[11], 71), 0),
    }


kernel_norm = 21.0 / (2.0 * math.pi)
face_width = 32.0
cell_height = 0.5
bondi_coef = 0.04
edd_coef = 0.25
step_dt = 0.05
feed_coef = 20.0
heat_coef = 10.0 / 9.0

def nearest(delta, length):
    half = 0.5 * length
    return jnp.where(delta > half, delta - length, jnp.where(delta < -half, delta + length, delta))

def block_density(rows, cols, z_length):
    delta_x = rows[0][:, None] - cols[0][None, :]
    delta_y = rows[1][:, None] - cols[1][None, :]
    delta_z = nearest(rows[2][:, None] - cols[2][None, :], z_length)
    smooth = 0.5 * (rows[4][:, None] + cols[4][None, :])
    ratio = jnp.sqrt(delta_x * delta_x + delta_y * delta_y + delta_z * delta_z) / smooth
    rest = jnp.maximum(1.0 - ratio, 0.0)
    kernel = kernel_norm / (smooth * smooth * smooth) * (rest * rest) * (rest * rest) * (1.0 + 4.0 * ratio)
    return lax.optimization_barrier(jnp.sum(kernel * cols[3][None, :], axis=1))

def domain_density(cells, pairs, z_length):

    def own_cell(cell_id):
        block = lax.dynamic_index_in_dim(cells, cell_id + BND, 1, keepdims=False)
        return block_density(block, block, z_length)
    start = lax.map(own_cell, jnp.arange(CPD, dtype=jnp.int32))

    def add_pair(step, total):
        home = pairs[0, step]
        other = pairs[1, step]
        rows = lax.dynamic_index_in_dim(cells, home + BND, 1, keepdims=False)
        cols = lax.dynamic_index_in_dim(cells, other, 1, keepdims=False)
        return total.at[home].add(block_density(rows, cols, z_length))
    return lax.fori_loop(0, NPAIR, add_pair, start)

def entry_terms(gas, hole, live, y_length, z_length):
    delta_x = gas[0] - hole[0]
    delta_y = nearest(gas[1] - hole[1], y_length)
    delta_z = nearest(gas[2] - hole[2], z_length)
    spread_sq = (delta_x * delta_x + delta_y * delta_y + delta_z * delta_z) / (hole[7] * hole[7])
    soft = 1.0 / (1.0 + spread_sq)
    weight = jnp.where(live, soft * soft, 0.0)
    mass_w = gas[6] * weight
    volume = weight * gas[6] / jnp.where(live, gas[8], 1.0)
    return jnp.stack([mass_w, mass_w * gas[7], mass_w * gas[3], mass_w * gas[4], mass_w * gas[5], volume])

def hole_rates(sums, hole_vel, hole_mass):
    mass_sum = sums[0]
    mean_heat = sums[1] / mass_sum
    drift = hole_vel - sums[2:5] / mass_sum[None]
    speed_sq = heat_coef * mean_heat + lax.optimization_barrier(jnp.sum(drift * drift, axis=0))
    rho_hole = mass_sum / sums[5]
    bondi = bondi_coef * hole_mass * hole_mass * rho_hole / (speed_sq * jnp.sqrt(speed_sq))
    limit = edd_coef * hole_mass
    rate = jnp.minimum(bondi, limit)
    return (rate, rate / limit, rho_hole)

def reference(gas_core, gas_vel, gas_energy, cell_pairs, bh_coord, bh_vel, bh_mass, bh_soft, mem_gas, mem_slot, send_count):
    devices_all = N_DX * N_DY * N_DZ
    group = N_DY * N_DZ
    local = CPD * CELL
    rim = BND * CELL
    z_length = cell_height * CPD * N_DZ
    y_length = face_width * N_DY
    core = gas_core.reshape(5, N_DX, N_DY, N_DZ, local)
    lower = jnp.roll(core, 1, axis=3)[..., local - rim:]
    upper = jnp.roll(core, -1, axis=3)[..., :rim]
    extended = jnp.concatenate([lower, core, upper], axis=4)
    extended = jnp.moveaxis(extended.reshape(5, devices_all, CPD + 2 * BND, CELL), 1, 0)
    pairs = jnp.moveaxis(cell_pairs.reshape(2, devices_all, NPAIR), 1, 0)
    batch = math.gcd(devices_all, 64)
    ext_batches = extended.reshape(devices_all // batch, batch, 5, CPD + 2 * BND, CELL)
    pair_batches = pairs.reshape(devices_all // batch, batch, 2, NPAIR)

    def one_batch(item):
        return jax.vmap(lambda cells, plist: domain_density(cells, plist, z_length))(item[0], item[1])
    dens = lax.map(one_batch, (ext_batches, pair_batches))
    density = dens.reshape(N_DX, N_DY, N_DZ * local)
    fields = jnp.concatenate([gas_core[0:3], gas_vel, gas_core[3:4], gas_energy[None], density[None]], 0)
    fields = fields.reshape(9, N_DX, group, local)
    index = mem_gas.reshape(N_DX, group, group * CAP)
    picked = jnp.take_along_axis(fields, jnp.broadcast_to(index[None], (9, N_DX, group, group * CAP)), axis=3)
    count = send_count.reshape(N_DX, group, group)
    live = (jnp.arange(CAP, dtype=jnp.int32)[None, None, None, :] < count[..., None]).reshape(N_DX, group, group * CAP)
    slot = mem_slot.reshape(N_DX, group, group * CAP)
    owner = jnp.arange(group * CAP, dtype=jnp.int32) // CAP
    target = owner[None, None, :] * NB + slot
    total = N_DX * group * NB
    hole_all = jnp.concatenate([bh_coord, bh_vel, bh_mass[None], bh_soft[None]], 0).reshape(8, total)
    segment = jnp.arange(N_DX, dtype=jnp.int32)[:, None, None] * (group * NB) + target
    segment = segment.reshape(-1)
    hole = jnp.take(hole_all, segment, axis=1).reshape(8, N_DX, group, group * CAP)
    terms = entry_terms(picked, hole, live, y_length, z_length)
    sums = jax.ops.segment_sum(terms.reshape(6, -1).T, segment, num_segments=total).T
    rate, ratio, rho_hole = hole_rates(sums, hole_all[3:6], hole_all[6])
    gain = step_dt * rate
    heat_gain = feed_coef * gain
    share = terms[5].reshape(-1) / jnp.take(sums[5], segment)
    lost_entry = jnp.take(gain, segment) * share
    heat_entry = jnp.take(heat_gain, segment) * share
    base = (jnp.arange(N_DX, dtype=jnp.int32)[:, None, None] * group + jnp.arange(group, dtype=jnp.int32)[None, :, None]) * local
    gas_id = (base + index).reshape(-1)
    lost = jax.ops.segment_sum(lost_entry, gas_id, num_segments=N_DX * group * local).reshape(N_DX, N_DY, N_DZ * local)
    heated = jax.ops.segment_sum(heat_entry, gas_id, num_segments=N_DX * group * local).reshape(N_DX, N_DY, N_DZ * local)
    mass = gas_core[3]
    gas_update = jnp.stack([mass - lost, gas_energy + heated / mass])
    bh_update = jnp.stack([ratio, rho_hole]).reshape(2, N_DX, N_DY, N_DZ * NB)
    return (density, gas_update, bh_update)
```

```python
import functools
import math

import jax
import jax.numpy as jnp
from jax import lax
from jax.experimental import pallas as pl
from jax.experimental.pallas import tpu as pltpu
from jax.sharding import PartitionSpec as P

CELL = 512
CPD = 16
BND = 10
NPAIR = 16
CAP = 24
LANES = 128
GROUPS = CELL // LANES
ROWS = CPD * GROUPS
REACH = BND * GROUPS
NEAR = 16
UNROLL = 16

kernel_norm = 21.0 / (2.0 * math.pi)
face_width = 32.0
cell_height = 0.5
bondi_coef = 0.04
edd_coef = 0.25
step_dt = 0.05
feed_coef = 20.0
heat_coef = 10.0 / 9.0
tiny = 1e-37


def vmem():
    return pl.BlockSpec(memory_space=pltpu.VMEM)


def nearest(delta, length):
    half = 0.5 * length
    return jnp.where(delta > half, delta - length, jnp.where(delta < -half, delta + length, delta))


def pair_term(p, q, wrap):
    dx = p[0] - q[0]
    dy = p[1] - q[1]
    dz = p[2] - q[2]
    if wrap is not None:
        dz = jnp.abs(dz)
        dz = jnp.minimum(dz, wrap - dz)
    dist_sq = jnp.maximum(dx * dx + dy * dy + dz * dz, tiny)
    smooth = p[3] + q[3]
    inverse = lax.rsqrt(smooth * smooth)
    rest = jnp.maximum(1.0 - (dist_sq * lax.rsqrt(dist_sq)) * inverse, 0.0)
    scaled = rest * inverse
    return (scaled * scaled) * (scaled * (rest * (1.25 - rest)))


def block_density(cols, rows, wrap):
    def step(turn, total):
        total = list(total)
        for inner in range(UNROLL):
            start = pl.multiple_of((turn * UNROLL + inner) * 8, 8)
            tile = cols[pl.ds(start, 8), :]
            q = [jnp.broadcast_to(tile[:, f : f + 1], (8, LANES)) for f in range(5)]
            for g in range(GROUPS):
                total[g] = total[g] + pair_term(rows[g], q, wrap) * q[4]
        return tuple(total)

    zero = jnp.zeros((8, LANES), jnp.float32)
    total = lax.fori_loop(0, CELL // 8 // UNROLL, step, (zero,) * GROUPS)
    summed = jnp.concatenate([jnp.sum(t, axis=0, keepdims=True) for t in total], axis=0)
    return summed * (4.0 * kernel_norm)


def cell_rows(cell):
    return pl.ds(pl.multiple_of(cell * GROUPS, GROUPS), GROUPS)


def load_cell(ref, cell):
    x, y, z, mass, smooth = [ref[f, cell_rows(cell), :] for f in range(5)]
    return [x, y, z, 0.5 * smooth, mass]


def fill_cols(cols, fields):
    for g in range(GROUPS):
        stack = [f[g : g + 1] for f in fields] + [jnp.zeros((3, LANES), jnp.float32)]
        cols[g * LANES : (g + 1) * LANES, 0:8] = jnp.concatenate(stack, axis=0).T


def spread_rows(fields):
    return [[jnp.broadcast_to(f[g : g + 1], (8, LANES)) for f in fields[:4]] for g in range(GROUPS)]


def span(z):
    return jnp.min(z), jnp.max(z)


def own_kernel(z_length, core_ref, out_ref, cols):
    def run(wrap):
        @pl.loop(0, CPD)
        def _(cell):
            fields = load_cell(core_ref, cell)
            fill_cols(cols, fields)
            out_ref[cell_rows(cell), :] = block_density(cols, spread_rows(fields), wrap)

    low, high = span(core_ref[2])
    near = high - low <= 0.5 * z_length
    pl.when(near)(lambda: run(None))
    pl.when(jnp.logical_not(near))(lambda: run(z_length))


def own_density(core, z_length):
    return pl.pallas_call(
        functools.partial(own_kernel, z_length),
        out_shape=jax.ShapeDtypeStruct((ROWS, LANES), jnp.float32),
        in_specs=[vmem()],
        out_specs=vmem(),
        scratch_shapes=[pltpu.VMEM((CELL, LANES), jnp.float32)],
        cost_estimate=pl.CostEstimate(flops=CPD * CELL * CELL * 26, bytes_accessed=200000, transcendentals=0),
        name="own_density",
    )(core)


def lane_take(values, lanes):
    return jnp.take_along_axis(values, lanes, axis=1, mode="promise_in_bounds")


def hole_rates(sums, hole_vel, hole_mass):
    mass_sum = sums[0]
    mean_heat = sums[1] / mass_sum
    drift = [v - s / mass_sum for v, s in zip(hole_vel, sums[2:5])]
    speed_sq = heat_coef * mean_heat + (drift[0] * drift[0] + drift[1] * drift[1] + drift[2] * drift[2])
    rho_hole = mass_sum / sums[5]
    bondi = bondi_coef * hole_mass * hole_mass * rho_hole / (speed_sq * jnp.sqrt(speed_sq))
    limit = edd_coef * hole_mass
    rate = jnp.minimum(bondi, limit)
    return rate, rate / limit, rho_hole


def feed_kernel(
    y_length,
    z_length,
    group,
    pairs_ref,
    core_ref,
    lower_ref,
    upper_ref,
    own_ref,
    vel_ref,
    energy_ref,
    gas_id_ref,
    slot_ref,
    count_ref,
    holes_ref,
    rho_ref,
    update_ref,
    message_ref,
    cells,
    cols,
):
    half = 0.5 * z_length
    low, high = span(core_ref[2])
    plain = high - low <= half
    edges = ((lower_ref, slice(ROWS - REACH, ROWS), 0), (upper_ref, slice(0, REACH), REACH + ROWS))
    for ref, part, at in edges:
        z = ref[2, part, :]
        edge_low, edge_high = span(z)
        above = edge_low - high > half
        below = low - edge_high > half
        inside = jnp.logical_and(edge_high - low <= half, high - edge_low <= half)
        plain = jnp.logical_and(plain, jnp.logical_or(inside, jnp.logical_or(above, below)))
        shift = jnp.where(above, -z_length, jnp.where(below, z_length, 0.0))
        for f in (0, 1, 3, 4):
            cells[f, at : at + REACH, :] = ref[f, part, :]
        cells[2, at : at + REACH, :] = z + shift
    for f in range(5):
        cells[f, REACH : REACH + ROWS, :] = core_ref[f]
    rho_ref[...] = own_ref[...]

    def run(wrap):
        @pl.loop(0, NPAIR)
        def _(step):
            home = pairs_ref[step]
            other = pairs_ref[NPAIR + step]
            fill_cols(cols, load_cell(cells, other))
            rows = spread_rows(load_cell(core_ref, home))
            rho_ref[cell_rows(home), :] += block_density(cols, rows, wrap)

    pl.when(plain)(lambda: run(None))

    @pl.when(jnp.logical_not(plain))
    def _():
        for ref, part, at in edges:
            cells[2, at : at + REACH, :] = ref[2, part, :]
        run(z_length)

    lane = lax.broadcasted_iota(jnp.int32, (8, LANES), 1)
    sub = lax.broadcasted_iota(jnp.int32, (8, LANES), 0)
    coded = gas_id_ref[...] * LANES + slot_ref[...]
    turned = []
    for v in range(CAP // 8):
        place = CAP * lane + (8 * v + sub)
        place_row, place_lane = place >> 7, place & (LANES - 1)
        piece = jnp.zeros((8, LANES), jnp.int32)
        for r in range(CAP):
            row = jnp.broadcast_to(coded[r : r + 1], (8, LANES))
            piece = jnp.where(place_row == r, lane_take(row, place_lane), piece)
        turned.append(piece)
    count = count_ref[...]
    live = [(8 * v + sub) < count for v in range(CAP // 8)]
    gas_row = [t >> 14 for t in turned]
    gas_lane = [(t >> 7) & (LANES - 1) for t in turned]
    slot = [t & (LANES - 1) for t in turned]

    sources = [(core_ref, 0), (core_ref, 1), (core_ref, 2)] + [(vel_ref, 0), (vel_ref, 1), (vel_ref, 2)]
    sources = sources + [(core_ref, 3), (energy_ref, None), (rho_ref, None)]
    blocks = CAP // 8

    def gather(turn, picked):
        picked = list(picked)
        for inner in range(4):
            r = turn * 4 + inner
            for f, (ref, plane) in enumerate(sources):
                line = ref[pl.ds(r, 1), :] if plane is None else ref[plane, pl.ds(r, 1), :]
                line = jnp.broadcast_to(line, (8, LANES))
                for v in range(blocks):
                    at = f * blocks + v
                    picked[at] = jnp.where(gas_row[v] == r, lane_take(line, gas_lane[v]), picked[at])
        return tuple(picked)

    zero = jnp.zeros((8, LANES), jnp.float32)
    picked = lax.fori_loop(0, ROWS // 4, gather, (zero,) * (9 * blocks))
    gas = [jnp.concatenate(picked[f * blocks : (f + 1) * blocks], axis=0) for f in range(9)]
    live = jnp.concatenate([l.astype(jnp.int32) for l in live], axis=0) > 0
    slot = jnp.concatenate(slot, axis=0)
    gas_row = jnp.concatenate(gas_row, axis=0)
    gas_lane = jnp.concatenate(gas_lane, axis=0)

    first = slot[0:1]
    second = jnp.max(jnp.where(live & (slot != first), slot, -1), axis=0, keepdims=True)
    is_first = live & (slot == first)
    is_second = live & (slot != first)

    two = jnp.concatenate([first, jnp.maximum(second, 0)] * (LANES // 2), axis=0)
    chosen = two.astype(jnp.float32).T.astype(jnp.int32)
    wide_lane = lax.broadcasted_iota(jnp.int32, (LANES, LANES), 1)
    held = jnp.zeros((LANES, LANES), jnp.float32)
    for f in range(8):
        table = holes_ref[pl.ds(f, group, stride=8), :]
        held = jnp.where((wide_lane >> 1) == f, lane_take(table, chosen), held)
    held = held.T
    hole_first = [held[2 * f : 2 * f + 1] for f in range(8)]
    hole_second = [held[2 * f + 1 : 2 * f + 2] for f in range(8)]
    hole = [jnp.where(is_first, a, b) for a, b in zip(hole_first, hole_second)]

    delta_x = gas[0] - hole[0]
    delta_y = nearest(gas[1] - hole[1], y_length)
    delta_z = nearest(gas[2] - hole[2], z_length)
    spread_sq = (delta_x * delta_x + delta_y * delta_y + delta_z * delta_z) / (hole[7] * hole[7])
    soft = 1.0 / (1.0 + spread_sq)
    weight = jnp.where(live, soft * soft, 0.0)
    mass_w = gas[6] * weight
    volume = mass_w / jnp.where(live, gas[8], 1.0)
    terms = [mass_w, mass_w * gas[7], mass_w * gas[3], mass_w * gas[4], mass_w * gas[5], volume]

    def settle(mine, held_by):
        sums = [jnp.sum(jnp.where(mine, t, 0.0), axis=0, keepdims=True) for t in terms]
        rate, ratio, rho_hole = hole_rates(sums, held_by[3:6], held_by[6])
        return step_dt * rate, sums[5], ratio, rho_hole

    gain_a, volume_a, ratio_a, rho_a = settle(is_first, hole_first)
    gain_b, volume_b, ratio_b, rho_b = settle(is_second, hole_second)
    lost = jnp.where(is_first, gain_a, gain_b) * (volume / jnp.where(is_first, volume_a, volume_b))
    lost = jnp.where(live, lost, 0.0)

    has_a = count > 0
    has_b = second >= 0
    lines = [
        jnp.where(has_a, first.astype(jnp.float32), -1.0),
        jnp.where(has_a, ratio_a, 0.0),
        jnp.where(has_a, rho_a, 0.0),
        second.astype(jnp.float32),
        jnp.where(has_b, ratio_b, 0.0),
        jnp.where(has_b, rho_b, 0.0),
        jnp.zeros((2, LANES), jnp.float32),
    ]
    message_ref[...] = jnp.concatenate(lines, axis=0)

    high = lost.astype(jnp.bfloat16).astype(jnp.float32)
    mid = (lost - high).astype(jnp.bfloat16).astype(jnp.float32)
    low = (lost - high) - mid
    tall = lax.broadcasted_iota(jnp.int32, (LANES, LANES), 0)
    total = jnp.zeros((ROWS, 3 * LANES), jnp.float32)
    for k in range(CAP):
        at_row = (tall[:ROWS] == gas_row[k : k + 1]).astype(jnp.float32).astype(jnp.bfloat16)
        at_lane = tall == gas_lane[k : k + 1]
        parts = [jnp.where(at_lane, part[k : k + 1], 0.0).astype(jnp.bfloat16) for part in (high, mid, low)]
        total = total + lax.dot_general(
            at_row,
            jnp.concatenate(parts, axis=0),
            (((1,), (1,)), ((), ())),
            preferred_element_type=jnp.float32,
        )
    taken = total[:, 0:LANES] + total[:, LANES : 2 * LANES] + total[:, 2 * LANES :]
    mass = core_ref[3]
    update_ref[0] = mass - taken
    update_ref[1] = energy_ref[...] + feed_coef * taken / mass


def feed(pairs, core, lower, upper, own, vel, energy, gas_id, slot, count, holes, y_length, z_length, group):
    smem = pl.BlockSpec(memory_space=pltpu.SMEM)
    return pl.pallas_call(
        functools.partial(feed_kernel, y_length, z_length, group),
        out_shape=(
            jax.ShapeDtypeStruct((ROWS, LANES), jnp.float32),
            jax.ShapeDtypeStruct((2, ROWS, LANES), jnp.float32),
            jax.ShapeDtypeStruct((8, LANES), jnp.float32),
        ),
        in_specs=[smem] + [vmem()] * 10,
        out_specs=(vmem(),) * 3,
        scratch_shapes=[
            pltpu.VMEM((5, 2 * REACH + ROWS, LANES), jnp.float32),
            pltpu.VMEM((CELL, LANES), jnp.float32),
        ],
        cost_estimate=pl.CostEstimate(flops=NPAIR * CELL * CELL * 26, bytes_accessed=2000000, transcendentals=0),
        name="feed",
    )(pairs, core, lower, upper, own, vel, energy, gas_id, slot, count, holes)


def settle_kernel(group, arrived_ref, out_ref):
    lane = lax.broadcasted_iota(jnp.int32, (group, LANES), 1).astype(jnp.float32)
    parts = [jnp.broadcast_to(arrived_ref[:, f : f + 1], (group, LANES)) for f in range(6)]
    at_first = lane == parts[0]
    at_second = lane == parts[3]
    for k in range(2):
        value = jnp.where(at_first, parts[1 + k], jnp.where(at_second, parts[4 + k], 0.0))
        out_ref[k] = jnp.sum(value, axis=0, keepdims=True)


def settle(arrived, group):
    return pl.pallas_call(
        functools.partial(settle_kernel, group),
        out_shape=jax.ShapeDtypeStruct((2, 1, LANES), jnp.float32),
        in_specs=[vmem()],
        out_specs=vmem(),
        name="settle",
    )(arrived)


def body(gas_core, gas_vel, gas_energy, cell_pairs, bh_coord, bh_vel, bh_mass, bh_soft, mem_gas, mem_slot, send_count):
    group = lax.axis_size("dy") * lax.axis_size("dz")
    deep = lax.axis_size("dz")
    z_length = cell_height * CPD * deep
    y_length = face_width * lax.axis_size("dy")
    core = gas_core.reshape(5, ROWS, LANES)
    lower = lax.ppermute(core, "dz", [(i, (i + 1) % deep) for i in range(deep)])
    upper = lax.ppermute(core, "dz", [((i + 1) % deep, i) for i in range(deep)])
    table = jnp.concatenate(
        [bh_coord.reshape(3, LANES), bh_vel.reshape(3, LANES), bh_mass.reshape(1, LANES), bh_soft.reshape(1, LANES)], 0
    )
    copies = jnp.broadcast_to(table[None], (group, 8, LANES))
    holes = lax.all_to_all(copies, ("dy", "dz"), split_axis=0, concat_axis=0, tiled=True).reshape(group * 8, LANES)
    own = own_density(core, z_length)
    rho, update, message = feed(
        cell_pairs.reshape(2 * NPAIR),
        core,
        lower,
        upper,
        own,
        gas_vel.reshape(3, ROWS, LANES),
        gas_energy.reshape(ROWS, LANES),
        mem_gas.reshape(CAP, LANES),
        mem_slot.reshape(CAP, LANES),
        send_count.reshape(1, LANES),
        holes,
        y_length,
        z_length,
        group,
    )
    arrived = lax.all_to_all(message.T, ("dy", "dz"), split_axis=0, concat_axis=0, tiled=True)
    bh_update = settle(arrived, group)
    return (
        rho.reshape(1, 1, CPD * CELL),
        update.reshape(2, 1, 1, CPD * CELL),
        bh_update.reshape(2, 1, 1, LANES),
    )


def solution(mesh):
    lead, plain = P(None, "dx", "dy", "dz"), P("dx", "dy", "dz")
    in_specs = (lead, lead, plain, lead, lead, lead, plain, plain, plain, plain, plain)
    return jax.shard_map(body, mesh=mesh, in_specs=in_specs, out_specs=(plain, lead, lead), check_vma=False)
```

```python
import functools
import math

import jax
import jax.numpy as jnp
from jax import lax
from jax.experimental import pallas as pl
from jax.experimental.pallas import tpu as pltpu
from jax.sharding import PartitionSpec as P

CELL = 512
CPD = 16
BND = 10
NPAIR = 16
CAP = 24
LANES = 128
GROUPS = CELL // LANES
ROWS = CPD * GROUPS
REACH = BND * GROUPS
TILES = LANES // 8
BINS = 32768.0
UNROLL = 16

kernel_norm = 21.0 / (2.0 * math.pi)
face_width = 32.0
cell_height = 0.5
bondi_coef = 0.04
edd_coef = 0.25
step_dt = 0.05
feed_coef = 20.0
heat_coef = 10.0 / 9.0
tiny = 1e-37


def vmem():
    return pl.BlockSpec(memory_space=pltpu.VMEM)


def nearest(delta, length):
    half = 0.5 * length
    return jnp.where(delta > half, delta - length, jnp.where(delta < -half, delta + length, delta))


def pair_term(p, q, wrap):
    dx = p[0] - q[0]
    dy = p[1] - q[1]
    dz = p[2] - q[2]
    if wrap is not None:
        dz = jnp.abs(dz)
        dz = jnp.minimum(dz, wrap - dz)
    dist_sq = jnp.maximum(dx * dx + dy * dy + dz * dz, tiny)
    smooth = p[3] + q[3]
    inverse = lax.rsqrt(smooth * smooth)
    rest = jnp.maximum(1.0 - (dist_sq * lax.rsqrt(dist_sq)) * inverse, 0.0)
    scaled = rest * inverse
    return (scaled * scaled) * (scaled * (rest * (1.25 - rest)))


def load_cols(cols, tile):
    return [cols[f, pl.ds(pl.multiple_of(tile * 8, 8), 8), :] for f in range(5)]


def fold(parts):
    return jnp.sum(parts, axis=0, keepdims=True)


def dense_block(cols, rows, wrap):
    def step(turn, total):
        total = list(total)
        for inner in range(4):
            q = load_cols(cols, turn * 4 + inner)
            for g in range(GROUPS):
                total[g] = total[g] + pair_term(rows[g], q, wrap) * q[4]
        return tuple(total)

    zero = jnp.zeros((8, LANES), jnp.float32)
    return lax.fori_loop(0, CELL // 32, step, (zero,) * GROUPS)


def band_block(cols, rows):
    def step(turn, total):
        total = list(total)
        for h in range(GROUPS):
            for inner in range(UNROLL):
                q = load_cols(cols, h * TILES + turn * UNROLL + inner)
                for g in range(max(h - 1, 0), min(h + 2, GROUPS)):
                    total[g] = total[g] + pair_term(rows[g], q, None) * q[4]
        return tuple(total)

    zero = jnp.zeros((8, LANES), jnp.float32)
    return lax.fori_loop(0, TILES // UNROLL, step, (zero,) * GROUPS)


def mirror_block(cols, rows, mirror):
    def step(turn, total):
        total = list(total)
        for h in range(GROUPS):
            for inner in range(UNROLL):
                tile = turn * UNROLL + inner
                q = load_cols(cols, h * TILES + tile)
                total[h] = total[h] + pair_term(rows[h], q, None) * q[4]
                if h + 1 < GROUPS:
                    term = pair_term(rows[h + 1], q, None)
                    total[h + 1] = total[h + 1] + term * q[4]
                    mirror[pl.ds(pl.multiple_of((h * TILES + tile) * 8, 8), 8), :] = term * rows[h + 1][4]
        return tuple(total)

    zero = jnp.zeros((8, LANES), jnp.float32)
    total = list(lax.fori_loop(0, TILES // UNROLL, step, (zero,) * GROUPS))
    for h in range(GROUPS - 1):
        part = mirror[h * LANES : (h + 1) * LANES, :].T
        total[h] = total[h] + jnp.sum(part.reshape(TILES, 8, LANES), axis=0)
    return total


def corner_block(cols, row, h):
    def step(turn, total):
        for inner in range(4):
            q = load_cols(cols, h * TILES + turn * 4 + inner)
            total = total + pair_term(row, q, None) * q[4]
        return total

    return lax.fori_loop(0, TILES // 4, step, jnp.zeros((8, LANES), jnp.float32))


def cell_rows(cell):
    return pl.ds(pl.multiple_of(cell * GROUPS, GROUPS), GROUPS)


def load_cell(ref, cell):
    return [ref[f, cell_rows(cell), :] for f in range(5)]


def fill_cols(cols, fields):
    for g in range(GROUPS):
        for f in range(5):
            cols[f, g * LANES : (g + 1) * LANES, :] = jnp.broadcast_to(fields[f][g : g + 1], (LANES, LANES)).T


def spread_rows(fields):
    return [[jnp.broadcast_to(f[g : g + 1], (8, LANES)) for f in fields] for g in range(GROUPS)]


def put_total(out_ref, cell, total, add):
    summed = jnp.concatenate([fold(t) for t in total], axis=0) * (4.0 * kernel_norm)
    out_ref[cell_rows(cell), :] = out_ref[cell_rows(cell), :] + summed if add else summed


def far_groups(p_stat, p_cell, q_stat, q_cell):
    reach = p_stat[0, p_cell * GROUPS, 2] + q_stat[0, q_cell * GROUPS, 2]
    reach = reach * 1.0001
    found = []
    for g in range(GROUPS):
        for h in range(GROUPS):
            if abs(g - h) >= 2:
                p_low, p_high = p_stat[0, p_cell * GROUPS + g, 0], p_stat[0, p_cell * GROUPS + g, 1]
                q_low, q_high = q_stat[0, q_cell * GROUPS + h, 0], q_stat[0, q_cell * GROUPS + h, 1]
                near = jnp.logical_and(p_low - q_high <= reach, q_low - p_high <= reach)
                found.append((g, h, near))
    return found


def run_corners(out_ref, cell, cols, rows, found):
    for g, h, near in found:

        @pl.when(near)
        def _():
            part = fold(corner_block(cols, rows[g], h)) * (4.0 * kernel_norm)
            at = pl.ds(cell * GROUPS + g, 1)
            out_ref[at, :] = out_ref[at, :] + part


def span(z):
    return jnp.min(z), jnp.max(z)


def by_group(ref, plane, g):
    return ref[plane, pl.ds(g, CPD, stride=GROUPS), :]


def ordered(keys):
    depth = CELL // 8
    lane = lax.broadcasted_iota(jnp.int32, (8, LANES), 1)
    sub = lax.broadcasted_iota(jnp.int32, (8, LANES), 0)
    lane_of = {64: 64, 128: 1, 256: 2}

    def bit(step, block):
        if step < 8:
            return sub & step == 0
        if step < 64:
            return block * 8 & step == 0
        return None if step >= CELL else lane & lane_of[step] == 0

    def same(a, b):
        if isinstance(a, bool) and isinstance(b, bool):
            return a == b
        if isinstance(a, bool):
            a, b = b, a
        if isinstance(b, bool):
            return a if b else jnp.logical_not(a)
        return jnp.logical_not(jnp.logical_xor(a, b))

    size = 2
    while size <= CELL:
        gap = size // 2
        while gap >= 1:
            fresh = []
            for k in range(len(keys)):
                if gap >= 64:
                    other = lane_take(keys[k], lane ^ lane_of[gap])
                elif gap >= 8:
                    other = keys[k ^ (gap // 8)]
                else:
                    down = pltpu.roll(keys[k], gap, 0)
                    up = down if gap == 4 else pltpu.roll(keys[k], 8 - gap, 0)
                    other = up if gap == 4 else jnp.where(sub & gap == 0, up, down)
                rising = bit(size, k)
                keep = same(bit(gap, k), True if rising is None else rising)
                if isinstance(keep, bool):
                    fresh.append(jnp.minimum(keys[k], other) if keep else jnp.maximum(keys[k], other))
                else:
                    fresh.append(jnp.where(keep, jnp.minimum(keys[k], other), jnp.maximum(keys[k], other)))
            keys = fresh
            gap //= 2
        size *= 2
    return keys


def upright(rows):
    half = rows.T
    joined = jnp.concatenate([half[0:64], half[64:128]], axis=1)
    return [joined[8 * k : 8 * k + 8] for k in range(8)]


def flat(blocks):
    joined = jnp.concatenate(blocks, axis=0)
    return jnp.concatenate([joined[:, 0:64], joined[:, 64:128]], axis=0).T


def remainder(key):
    return key - jnp.floor(key * (1.0 / CELL)) * CELL


def order_kernel(core_ref, out_ref, back_ref, spare):
    lane = lax.broadcasted_iota(jnp.int32, (CPD, LANES), 1)
    x = [by_group(core_ref, 0, g) for g in range(GROUPS)]
    low = jnp.min(jnp.minimum(jnp.minimum(x[0], x[1]), jnp.minimum(x[2], x[3])), axis=1, keepdims=True)
    high = jnp.max(jnp.maximum(jnp.maximum(x[0], x[1]), jnp.maximum(x[2], x[3])), axis=1, keepdims=True)
    scale = (BINS - 1.0) / jnp.maximum(high - low, tiny)
    for g in range(GROUPS):
        bin_at = jnp.floor((x[g] - low) * scale)
        bin_at = jnp.where(bin_at > 0.0, jnp.minimum(bin_at, BINS - 1.0), 0.0)
        spare[pl.ds(g, CPD, stride=GROUPS), :] = bin_at * CELL + (lane + g * LANES).astype(jnp.float32)
    keys = ordered(upright(spare[...]))
    source = [remainder(k) for k in keys]
    spare[...] = flat(source)
    wide = lax.broadcasted_iota(jnp.int32, (8, LANES), 1)
    deep = lax.broadcasted_iota(jnp.int32, (8, LANES), 0)
    above = (wide & 3) * LANES + (wide >> 6) * 64 + deep
    places = [(above + 8 * k).astype(jnp.float32) for k in range(8)]
    back = ordered([s * CELL + p for s, p in zip(source, places)])
    back_ref[...] = flat([remainder(k) for k in back]).astype(jnp.int32)
    whole = [spare[pl.ds(g, CPD, stride=GROUPS), :].astype(jnp.int32) for g in range(GROUPS)]
    for f, plane in enumerate((0, 1, 2, 4, 3)):
        had = [by_group(core_ref, plane, g) for g in range(GROUPS)]
        if plane == 4:
            had = [0.5 * h for h in had]
        now = []
        for g in range(GROUPS):
            group_at, lane_at = whole[g] >> 7, whole[g] & (LANES - 1)
            value = lane_take(had[0], lane_at)
            for other in range(1, GROUPS):
                value = jnp.where(group_at == other, lane_take(had[other], lane_at), value)
            now.append(value)
            out_ref[f, pl.ds(g, CPD, stride=GROUPS), :] = value
        if plane == 0:
            lows = [jnp.min(v, axis=1, keepdims=True) for v in now]
            highs = [jnp.max(v, axis=1, keepdims=True) for v in now]
        if plane == 4:
            tops = jnp.max(jnp.maximum(jnp.maximum(now[0], now[1]), jnp.maximum(now[2], now[3])), axis=1, keepdims=True)
    for g in range(GROUPS):
        stat = jnp.where(lane == 0, lows[g], jnp.where(lane == 1, highs[g], tops))
        out_ref[5, pl.ds(g, CPD, stride=GROUPS), :] = stat


def order(core):
    return pl.pallas_call(
        order_kernel,
        out_shape=(
            jax.ShapeDtypeStruct((6, ROWS, LANES), jnp.float32),
            jax.ShapeDtypeStruct((ROWS, LANES), jnp.int32),
        ),
        in_specs=[vmem()],
        out_specs=(vmem(), vmem()),
        scratch_shapes=[pltpu.VMEM((ROWS, LANES), jnp.float32)],
        cost_estimate=pl.CostEstimate(flops=3000000, bytes_accessed=400000, transcendentals=0),
        name="order",
    )(core)


def own_kernel(z_length, stat_ref, core_ref, out_ref, cols, mirror):
    low, high = span(core_ref[2])
    plain = high - low <= 0.5 * z_length

    @pl.when(plain)
    def _():
        @pl.loop(0, CPD)
        def _(cell):
            fields = load_cell(core_ref, cell)
            fill_cols(cols, fields)
            rows = spread_rows(fields)
            put_total(out_ref, cell, mirror_block(cols, rows, mirror), False)
            run_corners(out_ref, cell, cols, rows, far_groups(stat_ref, cell, stat_ref, cell))

    @pl.when(jnp.logical_not(plain))
    def _():
        @pl.loop(0, CPD)
        def _(cell):
            fields = load_cell(core_ref, cell)
            fill_cols(cols, fields)
            put_total(out_ref, cell, dense_block(cols, spread_rows(fields), z_length), False)


def stat_spec():
    return pl.BlockSpec((1, ROWS, LANES), lambda i: (5, 0, 0), memory_space=pltpu.SMEM)


def own_density(core, z_length):
    return pl.pallas_call(
        functools.partial(own_kernel, z_length),
        out_shape=jax.ShapeDtypeStruct((ROWS, LANES), jnp.float32),
        in_specs=[stat_spec(), vmem()],
        out_specs=vmem(),
        scratch_shapes=[pltpu.VMEM((5, CELL, LANES), jnp.float32), pltpu.VMEM((CELL, LANES), jnp.float32)],
        cost_estimate=pl.CostEstimate(flops=CPD * CELL * CELL * 12, bytes_accessed=400000, transcendentals=0),
        grid=(1,),
        name="own_density",
    )(core, core)


def lane_take(values, lanes):
    return jnp.take_along_axis(values, lanes, axis=1, mode="promise_in_bounds")


def hole_rates(sums, hole_vel, hole_mass):
    mass_sum = sums[0]
    mean_heat = sums[1] / mass_sum
    drift = [v - s / mass_sum for v, s in zip(hole_vel, sums[2:5])]
    speed_sq = heat_coef * mean_heat + (drift[0] * drift[0] + drift[1] * drift[1] + drift[2] * drift[2])
    rho_hole = mass_sum / sums[5]
    bondi = bondi_coef * hole_mass * hole_mass * rho_hole / (speed_sq * jnp.sqrt(speed_sq))
    limit = edd_coef * hole_mass
    rate = jnp.minimum(bondi, limit)
    return rate, rate / limit, rho_hole


def feed_kernel(
    y_length,
    z_length,
    group,
    pairs_ref,
    stat_ref,
    lower_stat_ref,
    upper_stat_ref,
    sorted_ref,
    lower_ref,
    upper_ref,
    own_ref,
    back_ref,
    core_ref,
    vel_ref,
    energy_ref,
    gas_id_ref,
    slot_ref,
    count_ref,
    holes_ref,
    rho_ref,
    message_ref,
    lost_ref,
    gas_at_ref,
    cells,
    cols,
    held_rho,
):
    half = 0.5 * z_length
    low, high = span(sorted_ref[2])
    plain = high - low <= half
    edges = ((lower_ref, slice(ROWS - REACH, ROWS), 0), (upper_ref, slice(0, REACH), REACH + ROWS))
    for ref, part, at in edges:
        z = ref[2, part, :]
        edge_low, edge_high = span(z)
        above = edge_low - high > half
        below = low - edge_high > half
        inside = jnp.logical_and(edge_high - low <= half, high - edge_low <= half)
        plain = jnp.logical_and(plain, jnp.logical_or(inside, jnp.logical_or(above, below)))
        shift = jnp.where(above, -z_length, jnp.where(below, z_length, 0.0))
        for f in (0, 1, 3, 4):
            cells[f, at : at + REACH, :] = ref[f, part, :]
        cells[2, at : at + REACH, :] = z + shift
    for f in range(5):
        cells[f, REACH : REACH + ROWS, :] = sorted_ref[f]
    held_rho[...] = own_ref[...]

    @pl.when(plain)
    def _():
        @pl.loop(0, NPAIR)
        def _(step):
            home = pairs_ref[0, step]
            other = pairs_ref[1, step]
            fill_cols(cols, load_cell(cells, other))
            rows = spread_rows(load_cell(sorted_ref, home))
            put_total(held_rho, home, band_block(cols, rows), True)

            def corners(q_stat, q_cell):
                run_corners(held_rho, home, cols, rows, far_groups(stat_ref, home, q_stat, q_cell))

            pl.when(other < BND)(lambda: corners(lower_stat_ref, other + (CPD - BND)))
            pl.when(other >= BND + CPD)(lambda: corners(upper_stat_ref, other - (BND + CPD)))
            pl.when(jnp.logical_and(other >= BND, other < BND + CPD))(lambda: corners(stat_ref, other - BND))

    @pl.when(jnp.logical_not(plain))
    def _():
        for ref, part, at in edges:
            cells[2, at : at + REACH, :] = ref[2, part, :]

        @pl.loop(0, NPAIR)
        def _(step):
            home = pairs_ref[0, step]
            fill_cols(cols, load_cell(cells, pairs_ref[1, step]))
            rows = spread_rows(load_cell(sorted_ref, home))
            put_total(held_rho, home, dense_block(cols, rows, z_length), True)

    for g in range(GROUPS):
        back = back_ref[pl.ds(g, CPD, stride=GROUPS), :]
        group_at, lane_at = back >> 7, back & (LANES - 1)
        value = lane_take(held_rho[pl.ds(0, CPD, stride=GROUPS), :], lane_at)
        for other in range(1, GROUPS):
            moved = lane_take(held_rho[pl.ds(other, CPD, stride=GROUPS), :], lane_at)
            value = jnp.where(group_at == other, moved, value)
        rho_ref[pl.ds(g, CPD, stride=GROUPS), :] = value

    lane = lax.broadcasted_iota(jnp.int32, (8, LANES), 1)
    sub = lax.broadcasted_iota(jnp.int32, (8, LANES), 0)
    coded = gas_id_ref[...] * LANES + slot_ref[...]
    turned = []
    for v in range(CAP // 8):
        place = CAP * lane + (8 * v + sub)
        place_row, place_lane = place >> 7, place & (LANES - 1)
        piece = jnp.zeros((8, LANES), jnp.int32)
        for r in range(CAP):
            row = jnp.broadcast_to(coded[r : r + 1], (8, LANES))
            piece = jnp.where(place_row == r, lane_take(row, place_lane), piece)
        turned.append(piece)
    count = count_ref[...]
    live = [(8 * v + sub) < count for v in range(CAP // 8)]
    gas_row = [t >> 14 for t in turned]
    gas_lane = [(t >> 7) & (LANES - 1) for t in turned]
    slot = [t & (LANES - 1) for t in turned]

    sources = [(core_ref, 0), (core_ref, 1), (core_ref, 2)] + [(vel_ref, 0), (vel_ref, 1), (vel_ref, 2)]
    sources = sources + [(core_ref, 3), (energy_ref, None), (rho_ref, None)]
    blocks = CAP // 8

    def gather(turn, picked):
        picked = list(picked)
        for inner in range(4):
            r = turn * 4 + inner
            for f, (ref, plane) in enumerate(sources):
                line = ref[pl.ds(r, 1), :] if plane is None else ref[plane, pl.ds(r, 1), :]
                line = jnp.broadcast_to(line, (8, LANES))
                for v in range(blocks):
                    at = f * blocks + v
                    picked[at] = jnp.where(gas_row[v] == r, lane_take(line, gas_lane[v]), picked[at])
        return tuple(picked)

    zero = jnp.zeros((8, LANES), jnp.float32)
    picked = lax.fori_loop(0, ROWS // 4, gather, (zero,) * (9 * blocks))
    gas = [jnp.concatenate(picked[f * blocks : (f + 1) * blocks], axis=0) for f in range(9)]
    live = jnp.concatenate([l.astype(jnp.int32) for l in live], axis=0) > 0
    slot = jnp.concatenate(slot, axis=0)
    gas_row = jnp.concatenate(gas_row, axis=0)
    gas_lane = jnp.concatenate(gas_lane, axis=0)

    first = slot[0:1]
    second = jnp.max(jnp.where(live & (slot != first), slot, -1), axis=0, keepdims=True)
    is_first = live & (slot == first)
    is_second = live & (slot != first)

    two = jnp.concatenate([first, jnp.maximum(second, 0)] * (LANES // 2), axis=0)
    chosen = two.astype(jnp.float32).T.astype(jnp.int32)
    wide_lane = lax.broadcasted_iota(jnp.int32, (LANES, LANES), 1)
    held = jnp.zeros((LANES, LANES), jnp.float32)
    for f in range(8):
        table = holes_ref[pl.ds(f, group, stride=8), :]
        held = jnp.where((wide_lane >> 1) == f, lane_take(table, chosen), held)
    held = held.T
    hole_first = [held[2 * f : 2 * f + 1] for f in range(8)]
    hole_second = [held[2 * f + 1 : 2 * f + 2] for f in range(8)]
    hole = [jnp.where(is_first, a, b) for a, b in zip(hole_first, hole_second)]

    delta_x = gas[0] - hole[0]
    delta_y = nearest(gas[1] - hole[1], y_length)
    delta_z = nearest(gas[2] - hole[2], z_length)
    spread_sq = (delta_x * delta_x + delta_y * delta_y + delta_z * delta_z) / (hole[7] * hole[7])
    soft = 1.0 / (1.0 + spread_sq)
    weight = jnp.where(live, soft * soft, 0.0)
    mass_w = gas[6] * weight
    volume = mass_w / jnp.where(live, gas[8], 1.0)
    terms = [mass_w, mass_w * gas[7], mass_w * gas[3], mass_w * gas[4], mass_w * gas[5], volume]

    def settle(mine, held_by):
        sums = [jnp.sum(jnp.where(mine, t, 0.0), axis=0, keepdims=True) for t in terms]
        rate, ratio, rho_hole = hole_rates(sums, held_by[3:6], held_by[6])
        return step_dt * rate, sums[5], ratio, rho_hole

    gain_a, volume_a, ratio_a, rho_a = settle(is_first, hole_first)
    gain_b, volume_b, ratio_b, rho_b = settle(is_second, hole_second)
    lost = jnp.where(is_first, gain_a, gain_b) * (volume / jnp.where(is_first, volume_a, volume_b))
    lost = jnp.where(live, lost, 0.0)

    has_a = count > 0
    has_b = second >= 0
    lines = [
        jnp.where(has_a, first.astype(jnp.float32), -1.0),
        jnp.where(has_a, ratio_a, 0.0),
        jnp.where(has_a, rho_a, 0.0),
        second.astype(jnp.float32),
        jnp.where(has_b, ratio_b, 0.0),
        jnp.where(has_b, rho_b, 0.0),
        jnp.zeros((2, LANES), jnp.float32),
    ]
    lines = jnp.concatenate(lines + [jnp.zeros((LANES - 8, LANES), jnp.float32)], axis=0)
    message_ref[...] = lines.T[:, 0:8]
    lost_ref[...] = lost
    gas_at_ref[...] = gas_row * LANES + gas_lane


def feed(pairs, ranked, lower, upper, own, back, core, vel, energy, gas_id, slot, count, holes, y_length, z_length, group):
    smem = pl.BlockSpec(memory_space=pltpu.SMEM)
    return pl.pallas_call(
        functools.partial(feed_kernel, y_length, z_length, group),
        out_shape=(
            jax.ShapeDtypeStruct((ROWS, LANES), jnp.float32),
            jax.ShapeDtypeStruct((group, 8), jnp.float32),
            jax.ShapeDtypeStruct((CAP, LANES), jnp.float32),
            jax.ShapeDtypeStruct((CAP, LANES), jnp.int32),
        ),
        in_specs=[smem] + [stat_spec()] * 3 + [vmem()] * 12,
        out_specs=(vmem(),) * 4,
        scratch_shapes=[
            pltpu.VMEM((5, 2 * REACH + ROWS, LANES), jnp.float32),
            pltpu.VMEM((5, CELL, LANES), jnp.float32),
            pltpu.VMEM((ROWS, LANES), jnp.float32),
        ],
        cost_estimate=pl.CostEstimate(flops=NPAIR * CELL * CELL * 17, bytes_accessed=2000000, transcendentals=0),
        grid=(1,),
        name="feed",
    )(pairs, ranked, lower, upper, ranked, lower, upper, own, back, core, vel, energy, gas_id, slot, count, holes)


def apply_kernel(lost_ref, gas_at_ref, core_ref, energy_ref, update_ref):
    lost = lost_ref[...]
    gas_row, gas_lane = gas_at_ref[...] >> 7, gas_at_ref[...] & (LANES - 1)
    high = lost.astype(jnp.bfloat16).astype(jnp.float32)
    mid = (lost - high).astype(jnp.bfloat16).astype(jnp.float32)
    low = (lost - high) - mid
    tall = lax.broadcasted_iota(jnp.int32, (LANES, LANES), 0)
    total = jnp.zeros((ROWS, 3 * LANES), jnp.float32)
    for k in range(CAP):
        at_row = (tall[:ROWS] == gas_row[k : k + 1]).astype(jnp.float32).astype(jnp.bfloat16)
        at_lane = tall == gas_lane[k : k + 1]
        parts = [jnp.where(at_lane, part[k : k + 1], 0.0).astype(jnp.bfloat16) for part in (high, mid, low)]
        total = total + lax.dot_general(
            at_row,
            jnp.concatenate(parts, axis=0),
            (((1,), (1,)), ((), ())),
            preferred_element_type=jnp.float32,
        )
    taken = total[:, 0:LANES] + total[:, LANES : 2 * LANES] + total[:, 2 * LANES :]
    mass = core_ref[0]
    update_ref[0] = mass - taken
    update_ref[1] = energy_ref[...] + feed_coef * taken / mass


def apply(lost, gas_at, core, energy):
    mass_spec = pl.BlockSpec((1, ROWS, LANES), lambda i: (3, 0, 0), memory_space=pltpu.VMEM)
    return pl.pallas_call(
        apply_kernel,
        out_shape=jax.ShapeDtypeStruct((2, ROWS, LANES), jnp.float32),
        in_specs=[vmem(), vmem(), mass_spec, vmem()],
        out_specs=vmem(),
        cost_estimate=pl.CostEstimate(flops=1000000, bytes_accessed=100000, transcendentals=0),
        grid=(1,),
        name="apply",
    )(lost, gas_at, core, energy)


def settle_kernel(group, arrived_ref, out_ref):
    lane = lax.broadcasted_iota(jnp.int32, (group, LANES), 1).astype(jnp.float32)
    parts = [jnp.broadcast_to(arrived_ref[:, f : f + 1], (group, LANES)) for f in range(6)]
    at_first = lane == parts[0]
    at_second = lane == parts[3]
    for k in range(2):
        value = jnp.where(at_first, parts[1 + k], jnp.where(at_second, parts[4 + k], 0.0))
        out_ref[k] = jnp.sum(value, axis=0, keepdims=True)


def settle(arrived, group):
    return pl.pallas_call(
        functools.partial(settle_kernel, group),
        out_shape=jax.ShapeDtypeStruct((2, 1, LANES), jnp.float32),
        in_specs=[vmem()],
        out_specs=vmem(),
        name="settle",
    )(arrived)


def body(gas_core, gas_vel, gas_energy, cell_pairs, bh_coord, bh_vel, bh_mass, bh_soft, mem_gas, mem_slot, send_count):
    group = lax.axis_size("dy") * lax.axis_size("dz")
    deep = lax.axis_size("dz")
    z_length = cell_height * CPD * deep
    y_length = face_width * lax.axis_size("dy")
    core = gas_core.reshape(5, ROWS, LANES)
    energy = gas_energy.reshape(ROWS, LANES)
    ranked, back = order(core)
    lower = lax.ppermute(ranked, "dz", [(i, (i + 1) % deep) for i in range(deep)])
    upper = lax.ppermute(ranked, "dz", [((i + 1) % deep, i) for i in range(deep)])
    table = jnp.concatenate(
        [bh_coord.reshape(3, LANES), bh_vel.reshape(3, LANES), bh_mass.reshape(1, LANES), bh_soft.reshape(1, LANES)], 0
    )
    copies = jnp.broadcast_to(table[None], (group, 8, LANES))
    holes = lax.all_to_all(copies, ("dy", "dz"), split_axis=0, concat_axis=0, tiled=True).reshape(group * 8, LANES)
    own = own_density(ranked, z_length)
    rho, message, lost, gas_at = feed(
        cell_pairs.reshape(2, NPAIR),
        ranked,
        lower,
        upper,
        own,
        back,
        core,
        gas_vel.reshape(3, ROWS, LANES),
        energy,
        mem_gas.reshape(CAP, LANES),
        mem_slot.reshape(CAP, LANES),
        send_count.reshape(1, LANES),
        holes,
        y_length,
        z_length,
        group,
    )
    arrived = lax.all_to_all(message, ("dy", "dz"), split_axis=0, concat_axis=0, tiled=True)
    update = apply(lost, gas_at, core, energy)
    bh_update = settle(arrived, group)
    return (
        rho.reshape(1, 1, CPD * CELL),
        update.reshape(2, 1, 1, CPD * CELL),
        bh_update.reshape(2, 1, 1, LANES),
    )


def solution(mesh):
    lead, plain = P(None, "dx", "dy", "dz"), P("dx", "dy", "dz")
    in_specs = (lead, lead, plain, lead, lead, lead, plain, plain, plain, plain, plain)
    return jax.shard_map(body, mesh=mesh, in_specs=in_specs, out_specs=(plain, lead, lead), check_vma=False)
```

```python
import functools
import math

import jax
import jax.numpy as jnp
from jax import lax
from jax.experimental import pallas as pl
from jax.experimental.pallas import tpu as pltpu
from jax.sharding import PartitionSpec as P

CELL = 512
CPD = 16
BND = 10
NPAIR = 16
CAP = 24
LANES = 128
GROUPS = CELL // LANES
ROWS = CPD * GROUPS
REACH = BND * GROUPS
TILES = LANES // 8
BINS = 32768.0
UNROLL = 16
STATIC = 8
GRANT = 16 * 1024 * 1024

kernel_norm = 21.0 / (2.0 * math.pi)
face_width = 32.0
cell_height = 0.5
bondi_coef = 0.04
edd_coef = 0.25
step_dt = 0.05
feed_coef = 20.0
heat_coef = 10.0 / 9.0
tiny = 1e-37


def vmem():
    return pl.BlockSpec(memory_space=pltpu.VMEM)


def nearest(delta, length):
    half = 0.5 * length
    return jnp.where(delta > half, delta - length, jnp.where(delta < -half, delta + length, delta))


def pair_term(p, q, wrap):
    dx = p[0] - q[0]
    dy = p[1] - q[1]
    dz = p[2] - q[2]
    if wrap is not None:
        dz = jnp.abs(dz)
        dz = jnp.minimum(dz, wrap - dz)
    dist_sq = jnp.maximum(dx * dx + dy * dy + dz * dz, tiny)
    smooth = p[3] + q[3]
    inverse = lax.rsqrt(smooth * smooth)
    rest = jnp.maximum(1.0 - (dist_sq * lax.rsqrt(dist_sq)) * inverse, 0.0)
    scaled = rest * inverse
    return (scaled * scaled) * (scaled * (rest * (1.25 - rest)))


def load_cols(cols, tile):
    return [cols[f, pl.ds(pl.multiple_of(tile * 8, 8), 8), :] for f in range(5)]


def fold(parts):
    return jnp.sum(parts, axis=0, keepdims=True)


def dense_block(cols, rows, wrap):
    def step(turn, total):
        total = list(total)
        for inner in range(4):
            q = load_cols(cols, turn * 4 + inner)
            for g in range(GROUPS):
                total[g] = total[g] + pair_term(rows[g], q, wrap) * q[4]
        return tuple(total)

    zero = jnp.zeros((8, LANES), jnp.float32)
    return lax.fori_loop(0, CELL // 32, step, (zero,) * GROUPS)


def band_block(cols, rows):
    def step(turn, total):
        total = list(total)
        for h in range(GROUPS):
            for inner in range(UNROLL):
                q = load_cols(cols, h * TILES + turn * UNROLL + inner)
                for g in range(max(h - 1, 0), min(h + 2, GROUPS)):
                    total[g] = total[g] + pair_term(rows[g], q, None) * q[4]
        return tuple(total)

    zero = jnp.zeros((8, LANES), jnp.float32)
    return lax.fori_loop(0, TILES // UNROLL, step, (zero,) * GROUPS)


def mirror_block(cols, rows, mirror):
    def step(turn, total):
        total = list(total)
        for h in range(GROUPS):
            for inner in range(UNROLL):
                tile = turn * UNROLL + inner
                q = load_cols(cols, h * TILES + tile)
                total[h] = total[h] + pair_term(rows[h], q, None) * q[4]
                if h + 1 < GROUPS:
                    term = pair_term(rows[h + 1], q, None)
                    total[h + 1] = total[h + 1] + term * q[4]
                    mirror[pl.ds(pl.multiple_of((h * TILES + tile) * 8, 8), 8), :] = term * rows[h + 1][4]
        return tuple(total)

    zero = jnp.zeros((8, LANES), jnp.float32)
    total = list(lax.fori_loop(0, TILES // UNROLL, step, (zero,) * GROUPS))
    for h in range(GROUPS - 1):
        part = mirror[h * LANES : (h + 1) * LANES, :].T
        total[h] = total[h] + jnp.sum(part.reshape(TILES, 8, LANES), axis=0)
    return total


def corner_block(cols, row, h):
    def step(turn, total):
        for inner in range(4):
            q = load_cols(cols, h * TILES + turn * 4 + inner)
            total = total + pair_term(row, q, None) * q[4]
        return total

    return lax.fori_loop(0, TILES // 4, step, jnp.zeros((8, LANES), jnp.float32))


def cell_rows(cell):
    return pl.ds(pl.multiple_of(cell * GROUPS, GROUPS), GROUPS)


def load_cell(ref, cell):
    return [ref[f, cell_rows(cell), :] for f in range(5)]


def fill_cols(cols, fields):
    for g in range(GROUPS):
        for f in range(5):
            cols[f, g * LANES : (g + 1) * LANES, :] = jnp.broadcast_to(fields[f][g : g + 1], (LANES, LANES)).T


def spread_rows(fields):
    return [[jnp.broadcast_to(f[g : g + 1], (8, LANES)) for f in fields] for g in range(GROUPS)]


def put_total(out_ref, cell, total, add):
    summed = jnp.concatenate([fold(t) for t in total], axis=0) * (4.0 * kernel_norm)
    out_ref[cell_rows(cell), :] = out_ref[cell_rows(cell), :] + summed if add else summed


def far_groups(p_stat, p_cell, q_stat, q_cell):
    reach = p_stat[0, p_cell * GROUPS, 2] + q_stat[0, q_cell * GROUPS, 2]
    reach = reach * 1.0001
    found = []
    for g in range(GROUPS):
        for h in range(GROUPS):
            if abs(g - h) >= 2:
                p_low, p_high = p_stat[0, p_cell * GROUPS + g, 0], p_stat[0, p_cell * GROUPS + g, 1]
                q_low, q_high = q_stat[0, q_cell * GROUPS + h, 0], q_stat[0, q_cell * GROUPS + h, 1]
                near = jnp.logical_and(p_low - q_high <= reach, q_low - p_high <= reach)
                found.append((g, h, near))
    return found


def run_corners(out_ref, cell, cols, rows, found):
    some = functools.reduce(jnp.logical_or, [near for _, _, near in found])

    @pl.when(some)
    def _():
        for g, h, near in found:

            @pl.when(near)
            def _():
                part = fold(corner_block(cols, rows[g], h)) * (4.0 * kernel_norm)
                at = pl.ds(cell * GROUPS + g, 1)
                out_ref[at, :] = out_ref[at, :] + part


def span(z):
    return jnp.min(z), jnp.max(z)


def by_group(ref, plane, g):
    return ref[plane, pl.ds(g, CPD, stride=GROUPS), :]


def ordered(keys):
    depth = CELL // 8
    lane = lax.broadcasted_iota(jnp.int32, (8, LANES), 1)
    sub = lax.broadcasted_iota(jnp.int32, (8, LANES), 0)
    lane_of = {64: 64, 128: 1, 256: 2}

    def bit(step, block):
        if step < 8:
            return sub & step == 0
        if step < 64:
            return block * 8 & step == 0
        return None if step >= CELL else lane & lane_of[step] == 0

    def same(a, b):
        if isinstance(a, bool) and isinstance(b, bool):
            return a == b
        if isinstance(a, bool):
            a, b = b, a
        if isinstance(b, bool):
            return a if b else jnp.logical_not(a)
        return jnp.logical_not(jnp.logical_xor(a, b))

    size = 2
    while size <= CELL:
        gap = size // 2
        while gap >= 1:
            fresh = []
            for k in range(len(keys)):
                if gap >= 64:
                    other = lane_take(keys[k], lane ^ lane_of[gap])
                elif gap >= 8:
                    other = keys[k ^ (gap // 8)]
                else:
                    down = pltpu.roll(keys[k], gap, 0)
                    up = down if gap == 4 else pltpu.roll(keys[k], 8 - gap, 0)
                    other = up if gap == 4 else jnp.where(sub & gap == 0, up, down)
                rising = bit(size, k)
                keep = same(bit(gap, k), True if rising is None else rising)
                if isinstance(keep, bool):
                    fresh.append(jnp.minimum(keys[k], other) if keep else jnp.maximum(keys[k], other))
                else:
                    fresh.append(jnp.where(keep, jnp.minimum(keys[k], other), jnp.maximum(keys[k], other)))
            keys = fresh
            gap //= 2
        size *= 2
    return keys


def upright(rows):
    half = rows.T
    joined = jnp.concatenate([half[0:64], half[64:128]], axis=1)
    return [joined[8 * k : 8 * k + 8] for k in range(8)]


def flat(blocks):
    joined = jnp.concatenate(blocks, axis=0)
    return jnp.concatenate([joined[:, 0:64], joined[:, 64:128]], axis=0).T


def remainder(key):
    return key - jnp.floor(key * (1.0 / CELL)) * CELL


def order_kernel(core_ref, out_ref, back_ref, spare):
    lane = lax.broadcasted_iota(jnp.int32, (CPD, LANES), 1)
    x = [by_group(core_ref, 0, g) for g in range(GROUPS)]
    low = jnp.min(jnp.minimum(jnp.minimum(x[0], x[1]), jnp.minimum(x[2], x[3])), axis=1, keepdims=True)
    high = jnp.max(jnp.maximum(jnp.maximum(x[0], x[1]), jnp.maximum(x[2], x[3])), axis=1, keepdims=True)
    scale = (BINS - 1.0) / jnp.maximum(high - low, tiny)
    for g in range(GROUPS):
        bin_at = jnp.floor((x[g] - low) * scale)
        bin_at = jnp.where(bin_at > 0.0, jnp.minimum(bin_at, BINS - 1.0), 0.0)
        spare[pl.ds(g, CPD, stride=GROUPS), :] = bin_at * CELL + (lane + g * LANES).astype(jnp.float32)
    keys = ordered(upright(spare[...]))
    source = [remainder(k) for k in keys]
    spare[...] = flat(source)
    wide = lax.broadcasted_iota(jnp.int32, (8, LANES), 1)
    deep = lax.broadcasted_iota(jnp.int32, (8, LANES), 0)
    above = (wide & 3) * LANES + (wide >> 6) * 64 + deep
    places = [(above + 8 * k).astype(jnp.float32) for k in range(8)]
    back = ordered([s * CELL + p for s, p in zip(source, places)])
    back_ref[...] = flat([remainder(k) for k in back]).astype(jnp.int32)
    whole = [spare[pl.ds(g, CPD, stride=GROUPS), :].astype(jnp.int32) for g in range(GROUPS)]
    for f, plane in enumerate((0, 1, 2, 4, 3)):
        had = [by_group(core_ref, plane, g) for g in range(GROUPS)]
        if plane == 4:
            had = [0.5 * h for h in had]
        now = []
        for g in range(GROUPS):
            group_at, lane_at = whole[g] >> 7, whole[g] & (LANES - 1)
            value = lane_take(had[0], lane_at)
            for other in range(1, GROUPS):
                value = jnp.where(group_at == other, lane_take(had[other], lane_at), value)
            now.append(value)
            out_ref[f, pl.ds(g, CPD, stride=GROUPS), :] = value
        if plane == 0:
            lows = [jnp.min(v, axis=1, keepdims=True) for v in now]
            highs = [jnp.max(v, axis=1, keepdims=True) for v in now]
        if plane == 4:
            tops = jnp.max(jnp.maximum(jnp.maximum(now[0], now[1]), jnp.maximum(now[2], now[3])), axis=1, keepdims=True)
    for g in range(GROUPS):
        stat = jnp.where(lane == 0, lows[g], jnp.where(lane == 1, highs[g], tops))
        out_ref[5, pl.ds(g, CPD, stride=GROUPS), :] = stat


def order(core):
    return pl.pallas_call(
        order_kernel,
        out_shape=(
            jax.ShapeDtypeStruct((6, ROWS, LANES), jnp.float32),
            jax.ShapeDtypeStruct((ROWS, LANES), jnp.int32),
        ),
        in_specs=[vmem()],
        out_specs=(vmem(), vmem()),
        scratch_shapes=[pltpu.VMEM((ROWS, LANES), jnp.float32)],
        cost_estimate=pl.CostEstimate(flops=3000000, bytes_accessed=400000, transcendentals=0),
compiler_params=pltpu.CompilerParams(vmem_limit_bytes=GRANT),
        name="order",
    )(core)


def own_kernel(z_length, stat_ref, core_ref, out_ref, cols, mirror):
    low, high = span(core_ref[2])
    plain = high - low <= 0.5 * z_length

    @pl.when(plain)
    def _():
        @pl.loop(0, CPD)
        def _(cell):
            fields = load_cell(core_ref, cell)
            fill_cols(cols, fields)
            rows = spread_rows(fields)
            put_total(out_ref, cell, mirror_block(cols, rows, mirror), False)
            run_corners(out_ref, cell, cols, rows, far_groups(stat_ref, cell, stat_ref, cell))

    @pl.when(jnp.logical_not(plain))
    def _():
        @pl.loop(0, CPD)
        def _(cell):
            fields = load_cell(core_ref, cell)
            fill_cols(cols, fields)
            put_total(out_ref, cell, dense_block(cols, spread_rows(fields), z_length), False)


def stat_spec():
    return pl.BlockSpec((1, ROWS, LANES), lambda i: (5, 0, 0), memory_space=pltpu.SMEM)


def own_density(core, z_length):
    return pl.pallas_call(
        functools.partial(own_kernel, z_length),
        out_shape=jax.ShapeDtypeStruct((ROWS, LANES), jnp.float32),
        in_specs=[stat_spec(), vmem()],
        out_specs=vmem(),
        scratch_shapes=[pltpu.VMEM((5, CELL, LANES), jnp.float32), pltpu.VMEM((CELL, LANES), jnp.float32)],
        cost_estimate=pl.CostEstimate(flops=CPD * CELL * CELL * 12, bytes_accessed=400000, transcendentals=0),
        grid=(1,),
compiler_params=pltpu.CompilerParams(vmem_limit_bytes=GRANT),
        name="own_density",
    )(core, core)


def lane_take(values, lanes):
    return jnp.take_along_axis(values, lanes, axis=1, mode="promise_in_bounds")


def hole_rates(sums, hole_vel, hole_mass):
    mass_sum = sums[0]
    mean_heat = sums[1] / mass_sum
    drift = [v - s / mass_sum for v, s in zip(hole_vel, sums[2:5])]
    speed_sq = heat_coef * mean_heat + (drift[0] * drift[0] + drift[1] * drift[1] + drift[2] * drift[2])
    rho_hole = mass_sum / sums[5]
    bondi = bondi_coef * hole_mass * hole_mass * rho_hole / (speed_sq * jnp.sqrt(speed_sq))
    limit = edd_coef * hole_mass
    rate = jnp.minimum(bondi, limit)
    return rate, rate / limit, rho_hole


def pairs_kernel(
    z_length,
    pairs_ref,
    stat_ref,
    lower_stat_ref,
    upper_stat_ref,
    sorted_ref,
    lower_ref,
    upper_ref,
    own_ref,
    back_ref,
    core_ref,
    vel_ref,
    energy_ref,
    gas_id_ref,
    slot_ref,
    rho_ref,
    picked_ref,
    place_ref,
    cells,
    cols,
    held_rho,
):
    blocks = CAP // 8
    lane = lax.broadcasted_iota(jnp.int32, (8, LANES), 1)
    sub = lax.broadcasted_iota(jnp.int32, (8, LANES), 0)
    coded = gas_id_ref[...] * LANES + slot_ref[...]
    for v in range(blocks):
        place = CAP * lane + (8 * v + sub)
        place_row, place_lane = place >> 7, place & (LANES - 1)
        piece = jnp.zeros((8, LANES), jnp.int32)
        for r in range(CAP):
            row = jnp.broadcast_to(coded[r : r + 1], (8, LANES))
            piece = jnp.where(place_row == r, lane_take(row, place_lane), piece)
        place_ref[8 * v : 8 * v + 8, :] = piece
    sources = [(core_ref, 0), (core_ref, 1), (core_ref, 2)] + [(vel_ref, 0), (vel_ref, 1), (vel_ref, 2)]
    sources = sources + [(core_ref, 3), (energy_ref, 0)]
    per_step = ROWS // NPAIR

    def pick(first, lines):
        for v in range(blocks):
            part = slice(8 * v, 8 * v + 8)
            at = place_ref[part, :]
            gas_row, gas_lane = at >> 14, (at >> 7) & (LANES - 1)
            here = [gas_row == first + inner for inner in range(per_step)]
            for field, (ref, plane) in lines:
                value = picked_ref[field, part, :]
                for inner in range(per_step):
                    line = ref[pl.ds(first + inner, 1), :] if plane is None else ref[plane, pl.ds(first + inner, 1), :]
                    moved = lane_take(jnp.broadcast_to(line, (8, LANES)), gas_lane)
                    value = jnp.where(here[inner], moved, value)
                picked_ref[field, part, :] = value

    def pick_rows(step):
        pick(step * per_step, list(enumerate(sources)))

    half = 0.5 * z_length
    low, high = span(sorted_ref[2])
    plain = high - low <= half
    edges = ((lower_ref, slice(ROWS - REACH, ROWS), 0), (upper_ref, slice(0, REACH), REACH + ROWS))
    for ref, part, at in edges:
        z = ref[2, part, :]
        edge_low, edge_high = span(z)
        above = edge_low - high > half
        below = low - edge_high > half
        inside = jnp.logical_and(edge_high - low <= half, high - edge_low <= half)
        plain = jnp.logical_and(plain, jnp.logical_or(inside, jnp.logical_or(above, below)))
        shift = jnp.where(above, -z_length, jnp.where(below, z_length, 0.0))
        for f in (0, 1, 3, 4):
            cells[f, at : at + REACH, :] = ref[f, part, :]
        cells[2, at : at + REACH, :] = z + shift
    for f in range(5):
        cells[f, REACH : REACH + ROWS, :] = sorted_ref[f]
    held_rho[...] = own_ref[...]

    @pl.when(plain)
    def _():
        @pl.loop(0, NPAIR)
        def _(step):
            home = pairs_ref[0, step]
            other = pairs_ref[1, step]
            fill_cols(cols, load_cell(cells, other))
            rows = spread_rows(load_cell(sorted_ref, home))
            pick_rows(step)
            put_total(held_rho, home, band_block(cols, rows), True)

            def corners(q_stat, q_cell):
                run_corners(held_rho, home, cols, rows, far_groups(stat_ref, home, q_stat, q_cell))

            pl.when(other < BND)(lambda: corners(lower_stat_ref, other + (CPD - BND)))
            pl.when(other >= BND + CPD)(lambda: corners(upper_stat_ref, other - (BND + CPD)))
            pl.when(jnp.logical_and(other >= BND, other < BND + CPD))(lambda: corners(stat_ref, other - BND))

    @pl.when(jnp.logical_not(plain))
    def _():
        for ref, part, at in edges:
            cells[2, at : at + REACH, :] = ref[2, part, :]

        @pl.loop(0, NPAIR)
        def _(step):
            home = pairs_ref[0, step]
            fill_cols(cols, load_cell(cells, pairs_ref[1, step]))
            pick_rows(step)
            rows = spread_rows(load_cell(sorted_ref, home))
            put_total(held_rho, home, dense_block(cols, rows, z_length), True)

    for g in range(GROUPS):
        back = back_ref[pl.ds(g, CPD, stride=GROUPS), :]
        group_at, lane_at = back >> 7, back & (LANES - 1)
        value = lane_take(held_rho[pl.ds(0, CPD, stride=GROUPS), :], lane_at)
        for other in range(1, GROUPS):
            moved = lane_take(held_rho[pl.ds(other, CPD, stride=GROUPS), :], lane_at)
            value = jnp.where(group_at == other, moved, value)
        rho_ref[pl.ds(g, CPD, stride=GROUPS), :] = value

    for step in range(NPAIR):
        pick(step * per_step, [(STATIC, (rho_ref, None))])


def pairs_density(pairs, ranked, lower, upper, own, back, core, vel, energy, gas_id, slot, z_length):
    smem = pl.BlockSpec(memory_space=pltpu.SMEM)
    return pl.pallas_call(
        functools.partial(pairs_kernel, z_length),
        out_shape=(
            jax.ShapeDtypeStruct((ROWS, LANES), jnp.float32),
            jax.ShapeDtypeStruct((STATIC + 1, CAP, LANES), jnp.float32),
            jax.ShapeDtypeStruct((CAP, LANES), jnp.int32),
        ),
        in_specs=[smem] + [stat_spec()] * 3 + [vmem()] * 10,
        out_specs=(vmem(),) * 3,
        scratch_shapes=[
            pltpu.VMEM((5, 2 * REACH + ROWS, LANES), jnp.float32),
            pltpu.VMEM((5, CELL, LANES), jnp.float32),
            pltpu.VMEM((ROWS, LANES), jnp.float32),
        ],
        cost_estimate=pl.CostEstimate(flops=NPAIR * CELL * CELL * 17, bytes_accessed=2000000, transcendentals=0),
        grid=(1,),
compiler_params=pltpu.CompilerParams(vmem_limit_bytes=GRANT),
        name="pairs_density",
    )(pairs, ranked, lower, upper, ranked, lower, upper, own, back, core, vel, energy, gas_id, slot)


def feed_kernel(y_length, z_length, group, picked_ref, place_ref, count_ref, holes_ref, message_ref, lost_ref, gas_at_ref):
    gas = [picked_ref[f] for f in range(STATIC + 1)]
    place = place_ref[...]
    slot = place & (LANES - 1)
    count = count_ref[...]
    live = lax.broadcasted_iota(jnp.int32, (CAP, LANES), 0) < count

    first = slot[0:1]
    second = jnp.max(jnp.where(live & (slot != first), slot, -1), axis=0, keepdims=True)
    is_first = live & (slot == first)
    is_second = live & (slot != first)

    two = jnp.concatenate([first, jnp.maximum(second, 0)] * (LANES // 2), axis=0)
    chosen = two.astype(jnp.float32).T.astype(jnp.int32)
    wide_lane = lax.broadcasted_iota(jnp.int32, (LANES, LANES), 1)
    held = jnp.zeros((LANES, LANES), jnp.float32)
    for f in range(8):
        table = holes_ref[pl.ds(f, group, stride=8), :]
        held = jnp.where((wide_lane >> 1) == f, lane_take(table, chosen), held)
    held = held.T
    hole_first = [held[2 * f : 2 * f + 1] for f in range(8)]
    hole_second = [held[2 * f + 1 : 2 * f + 2] for f in range(8)]
    hole = [jnp.where(is_first, a, b) for a, b in zip(hole_first, hole_second)]

    delta_x = gas[0] - hole[0]
    delta_y = nearest(gas[1] - hole[1], y_length)
    delta_z = nearest(gas[2] - hole[2], z_length)
    spread_sq = (delta_x * delta_x + delta_y * delta_y + delta_z * delta_z) / (hole[7] * hole[7])
    soft = 1.0 / (1.0 + spread_sq)
    weight = jnp.where(live, soft * soft, 0.0)
    mass_w = gas[6] * weight
    volume = mass_w / jnp.where(live, gas[8], 1.0)
    terms = [mass_w, mass_w * gas[7], mass_w * gas[3], mass_w * gas[4], mass_w * gas[5], volume]

    def settle(mine, held_by):
        sums = [jnp.sum(jnp.where(mine, t, 0.0), axis=0, keepdims=True) for t in terms]
        rate, ratio, rho_hole = hole_rates(sums, held_by[3:6], held_by[6])
        return step_dt * rate, sums[5], ratio, rho_hole

    gain_a, volume_a, ratio_a, rho_a = settle(is_first, hole_first)
    gain_b, volume_b, ratio_b, rho_b = settle(is_second, hole_second)
    lost = jnp.where(is_first, gain_a, gain_b) * (volume / jnp.where(is_first, volume_a, volume_b))
    lost = jnp.where(live, lost, 0.0)

    has_a = count > 0
    has_b = second >= 0
    lines = [
        jnp.where(has_a, first.astype(jnp.float32), -1.0),
        jnp.where(has_a, ratio_a, 0.0),
        jnp.where(has_a, rho_a, 0.0),
        second.astype(jnp.float32),
        jnp.where(has_b, ratio_b, 0.0),
        jnp.where(has_b, rho_b, 0.0),
        jnp.zeros((2, LANES), jnp.float32),
    ]
    lines = jnp.concatenate(lines + [jnp.zeros((LANES - 8, LANES), jnp.float32)], axis=0)
    message_ref[...] = lines.T[:, 0:8]
    lost_ref[...] = lost
    gas_at_ref[...] = place >> 7


def feed(picked, place, count, holes, y_length, z_length, group):
    return pl.pallas_call(
        functools.partial(feed_kernel, y_length, z_length, group),
        out_shape=(
            jax.ShapeDtypeStruct((group, 8), jnp.float32),
            jax.ShapeDtypeStruct((CAP, LANES), jnp.float32),
            jax.ShapeDtypeStruct((CAP, LANES), jnp.int32),
        ),
        in_specs=[vmem()] * 4,
        out_specs=(vmem(),) * 3,
        cost_estimate=pl.CostEstimate(flops=1000000, bytes_accessed=1000000, transcendentals=0),
compiler_params=pltpu.CompilerParams(vmem_limit_bytes=GRANT),
        name="feed",
    )(picked, place, count, holes)


def apply_kernel(lost_ref, gas_at_ref, core_ref, energy_ref, update_ref):
    lost = lost_ref[...]
    gas_row, gas_lane = gas_at_ref[...] >> 7, gas_at_ref[...] & (LANES - 1)
    high = lost.astype(jnp.bfloat16).astype(jnp.float32)
    mid = (lost - high).astype(jnp.bfloat16).astype(jnp.float32)
    low = (lost - high) - mid
    tall = lax.broadcasted_iota(jnp.int32, (LANES, LANES), 0)
    total = jnp.zeros((ROWS, 3 * LANES), jnp.float32)
    for k in range(CAP):
        at_row = (tall[:ROWS] == gas_row[k : k + 1]).astype(jnp.float32).astype(jnp.bfloat16)
        at_lane = tall == gas_lane[k : k + 1]
        parts = [jnp.where(at_lane, part[k : k + 1], 0.0).astype(jnp.bfloat16) for part in (high, mid, low)]
        total = total + lax.dot_general(
            at_row,
            jnp.concatenate(parts, axis=0),
            (((1,), (1,)), ((), ())),
            preferred_element_type=jnp.float32,
        )
    taken = total[:, 0:LANES] + total[:, LANES : 2 * LANES] + total[:, 2 * LANES :]
    mass = core_ref[0]
    update_ref[0] = mass - taken
    update_ref[1] = energy_ref[...] + feed_coef * taken / mass


def apply(lost, gas_at, core, energy):
    mass_spec = pl.BlockSpec((1, ROWS, LANES), lambda i: (3, 0, 0), memory_space=pltpu.VMEM)
    return pl.pallas_call(
        apply_kernel,
        out_shape=jax.ShapeDtypeStruct((2, ROWS, LANES), jnp.float32),
        in_specs=[vmem(), vmem(), mass_spec, vmem()],
        out_specs=vmem(),
        cost_estimate=pl.CostEstimate(flops=1000000, bytes_accessed=100000, transcendentals=0),
        grid=(1,),
compiler_params=pltpu.CompilerParams(vmem_limit_bytes=GRANT),
        name="apply",
    )(lost, gas_at, core, energy)


def spread_kernel(group, coord_ref, vel_ref, mass_ref, soft_ref, out_ref):
    lines = [coord_ref[f] for f in range(3)] + [vel_ref[f] for f in range(3)] + [mass_ref[0], soft_ref[0]]
    out_ref[...] = jnp.broadcast_to(jnp.concatenate(lines, axis=0)[None], (group, 8, LANES))


def spread(coord, vel, mass, soft, group):
    return pl.pallas_call(
        functools.partial(spread_kernel, group),
        out_shape=jax.ShapeDtypeStruct((group, 8, LANES), jnp.float32),
        in_specs=[vmem()] * 4,
        out_specs=vmem(),
compiler_params=pltpu.CompilerParams(vmem_limit_bytes=GRANT),
        name="spread",
    )(coord, vel, mass, soft)


def settle_kernel(group, arrived_ref, out_ref):
    lane = lax.broadcasted_iota(jnp.int32, (group, LANES), 1).astype(jnp.float32)
    parts = [jnp.broadcast_to(arrived_ref[:, f : f + 1], (group, LANES)) for f in range(6)]
    at_first = lane == parts[0]
    at_second = lane == parts[3]
    for k in range(2):
        value = jnp.where(at_first, parts[1 + k], jnp.where(at_second, parts[4 + k], 0.0))
        out_ref[k] = jnp.sum(value, axis=0, keepdims=True)


def settle(arrived, group):
    return pl.pallas_call(
        functools.partial(settle_kernel, group),
        out_shape=jax.ShapeDtypeStruct((2, 1, LANES), jnp.float32),
        in_specs=[vmem()],
        out_specs=vmem(),
compiler_params=pltpu.CompilerParams(vmem_limit_bytes=GRANT),
        name="settle",
    )(arrived)


def body(gas_core, gas_vel, gas_energy, cell_pairs, bh_coord, bh_vel, bh_mass, bh_soft, mem_gas, mem_slot, send_count):
    group = lax.axis_size("dy") * lax.axis_size("dz")
    deep = lax.axis_size("dz")
    z_length = cell_height * CPD * deep
    y_length = face_width * lax.axis_size("dy")
    core = gas_core.reshape(5, ROWS, LANES)
    energy = gas_energy.reshape(ROWS, LANES)
    ranked, back = order(core)
    lower = lax.ppermute(ranked, "dz", [(i, (i + 1) % deep) for i in range(deep)])
    upper = lax.ppermute(ranked, "dz", [((i + 1) % deep, i) for i in range(deep)])
    copies = spread(
        bh_coord.reshape(3, 1, LANES),
        bh_vel.reshape(3, 1, LANES),
        bh_mass.reshape(1, 1, LANES),
        bh_soft.reshape(1, 1, LANES),
        group,
    )
    holes = lax.all_to_all(copies, ("dy", "dz"), split_axis=0, concat_axis=0, tiled=True).reshape(group * 8, LANES)
    own = own_density(ranked, z_length)
    rho, picked, place = pairs_density(
        cell_pairs.reshape(2, NPAIR),
        ranked,
        lower,
        upper,
        own,
        back,
        core,
        gas_vel.reshape(3, ROWS, LANES),
        energy.reshape(1, ROWS, LANES),
        mem_gas.reshape(CAP, LANES),
        mem_slot.reshape(CAP, LANES),
        z_length,
    )
    message, lost, gas_at = feed(picked, place, send_count.reshape(1, LANES), holes, y_length, z_length, group)
    arrived = lax.all_to_all(message, ("dy", "dz"), split_axis=0, concat_axis=0, tiled=True)
    update = apply(lost, gas_at, core, energy)
    bh_update = settle(arrived, group)
    return (
        rho.reshape(1, 1, CPD * CELL),
        update.reshape(2, 1, 1, CPD * CELL),
        bh_update.reshape(2, 1, 1, LANES),
    )


def solution(mesh):
    lead, plain = P(None, "dx", "dy", "dz"), P("dx", "dy", "dz")
    in_specs = (lead, lead, plain, lead, lead, lead, plain, plain, plain, plain, plain)
    return jax.shard_map(body, mesh=mesh, in_specs=in_specs, out_specs=(plain, lead, lead), check_vma=False)
```

```python
import functools
import math

import jax
import jax.numpy as jnp
from jax import lax
from jax.experimental import pallas as pl
from jax.experimental.pallas import tpu as pltpu
from jax.sharding import PartitionSpec as P

CELL = 512
CPD = 16
BND = 10
NPAIR = 16
CAP = 24
LANES = 128
GROUPS = CELL // LANES
ROWS = CPD * GROUPS
REACH = BND * GROUPS
TILES = LANES // 8
BINS = 32768.0
UNROLL = 16
STATIC = 8
GRANT = 16 * 1024 * 1024

kernel_norm = 21.0 / (2.0 * math.pi)
face_width = 32.0
cell_height = 0.5
bondi_coef = 0.04
edd_coef = 0.25
step_dt = 0.05
feed_coef = 20.0
heat_coef = 10.0 / 9.0
tiny = 1e-37


def vmem():
    return pl.BlockSpec(memory_space=pltpu.VMEM)


def nearest(delta, length):
    half = 0.5 * length
    return jnp.where(delta > half, delta - length, jnp.where(delta < -half, delta + length, delta))


def pair_term(p, q, wrap):
    dx = p[0] - q[0]
    dy = p[1] - q[1]
    dz = p[2] - q[2]
    if wrap is not None:
        dz = jnp.abs(dz)
        dz = jnp.minimum(dz, wrap - dz)
    dist_sq = jnp.maximum(dx * dx + dy * dy + dz * dz, tiny)
    smooth = p[3] + q[3]
    inverse = lax.rsqrt(smooth * smooth)
    rest = jnp.maximum(1.0 - (dist_sq * lax.rsqrt(dist_sq)) * inverse, 0.0)
    scaled = rest * inverse
    return (scaled * scaled) * (scaled * (rest * (1.25 - rest)))


def load_cols(cols, tile):
    return [cols[f, pl.ds(pl.multiple_of(tile * 8, 8), 8), :] for f in range(5)]


def fold(parts):
    return jnp.sum(parts, axis=0, keepdims=True)


def dense_block(cols, rows, wrap):
    def step(turn, total):
        total = list(total)
        for inner in range(4):
            q = load_cols(cols, turn * 4 + inner)
            for g in range(GROUPS):
                total[g] = total[g] + pair_term(rows[g], q, wrap) * q[4]
        return tuple(total)

    zero = jnp.zeros((8, LANES), jnp.float32)
    return lax.fori_loop(0, CELL // 32, step, (zero,) * GROUPS)


def band_block(cols, rows):
    def step(turn, total):
        total = list(total)
        for h in range(GROUPS):
            for inner in range(UNROLL):
                q = load_cols(cols, h * TILES + turn * UNROLL + inner)
                for g in range(max(h - 1, 0), min(h + 2, GROUPS)):
                    total[g] = total[g] + pair_term(rows[g], q, None) * q[4]
        return tuple(total)

    zero = jnp.zeros((8, LANES), jnp.float32)
    return lax.fori_loop(0, TILES // UNROLL, step, (zero,) * GROUPS)


def mirror_block(cols, rows, mirror):
    def step(turn, total):
        total = list(total)
        for h in range(GROUPS):
            for inner in range(UNROLL):
                tile = turn * UNROLL + inner
                q = load_cols(cols, h * TILES + tile)
                total[h] = total[h] + pair_term(rows[h], q, None) * q[4]
                if h + 1 < GROUPS:
                    term = pair_term(rows[h + 1], q, None)
                    total[h + 1] = total[h + 1] + term * q[4]
                    mirror[pl.ds(pl.multiple_of((h * TILES + tile) * 8, 8), 8), :] = term * rows[h + 1][4]
        return tuple(total)

    zero = jnp.zeros((8, LANES), jnp.float32)
    total = list(lax.fori_loop(0, TILES // UNROLL, step, (zero,) * GROUPS))
    for h in range(GROUPS - 1):
        part = mirror[h * LANES : (h + 1) * LANES, :].T
        total[h] = total[h] + jnp.sum(part.reshape(TILES, 8, LANES), axis=0)
    return total


def corner_block(cols, row, h):
    def step(turn, total):
        for inner in range(4):
            q = load_cols(cols, h * TILES + turn * 4 + inner)
            total = total + pair_term(row, q, None) * q[4]
        return total

    return lax.fori_loop(0, TILES // 4, step, jnp.zeros((8, LANES), jnp.float32))


def cell_rows(cell):
    return pl.ds(pl.multiple_of(cell * GROUPS, GROUPS), GROUPS)


def load_cell(ref, cell):
    return [ref[f, cell_rows(cell), :] for f in range(5)]


def fill_cols(cols, fields):
    for g in range(GROUPS):
        for f in range(5):
            cols[f, g * LANES : (g + 1) * LANES, :] = jnp.broadcast_to(fields[f][g : g + 1], (LANES, LANES)).T


def spread_rows(fields):
    return [[jnp.broadcast_to(f[g : g + 1], (8, LANES)) for f in fields] for g in range(GROUPS)]


def put_total(out_ref, cell, total, add):
    summed = jnp.concatenate([fold(t) for t in total], axis=0) * (4.0 * kernel_norm)
    out_ref[cell_rows(cell), :] = out_ref[cell_rows(cell), :] + summed if add else summed


def far_groups(p_stat, p_cell, q_stat, q_cell):
    reach = p_stat[0, p_cell * GROUPS, 2] + q_stat[0, q_cell * GROUPS, 2]
    reach = reach * 1.0001
    found = []
    for g in range(GROUPS):
        for h in range(GROUPS):
            if abs(g - h) >= 2:
                p_low, p_high = p_stat[0, p_cell * GROUPS + g, 0], p_stat[0, p_cell * GROUPS + g, 1]
                q_low, q_high = q_stat[0, q_cell * GROUPS + h, 0], q_stat[0, q_cell * GROUPS + h, 1]
                near = jnp.logical_and(p_low - q_high <= reach, q_low - p_high <= reach)
                found.append((g, h, near))
    return found


def run_corners(out_ref, cell, cols, rows, found):
    some = functools.reduce(jnp.logical_or, [near for _, _, near in found])

    @pl.when(some)
    def _():
        for g, h, near in found:

            @pl.when(near)
            def _():
                part = fold(corner_block(cols, rows[g], h)) * (4.0 * kernel_norm)
                at = pl.ds(cell * GROUPS + g, 1)
                out_ref[at, :] = out_ref[at, :] + part


def span(z):
    return jnp.min(z), jnp.max(z)


def by_group(ref, plane, g):
    return ref[plane, pl.ds(g, CPD, stride=GROUPS), :]


def ordered(keys):
    depth = CELL // 8
    lane = lax.broadcasted_iota(jnp.int32, (8, LANES), 1)
    sub = lax.broadcasted_iota(jnp.int32, (8, LANES), 0)
    lane_of = {64: 64, 128: 1, 256: 2}

    def bit(step, block):
        if step < 8:
            return sub & step == 0
        if step < 64:
            return block * 8 & step == 0
        return None if step >= CELL else lane & lane_of[step] == 0

    def same(a, b):
        if isinstance(a, bool) and isinstance(b, bool):
            return a == b
        if isinstance(a, bool):
            a, b = b, a
        if isinstance(b, bool):
            return a if b else jnp.logical_not(a)
        return jnp.logical_not(jnp.logical_xor(a, b))

    size = 2
    while size <= CELL:
        gap = size // 2
        while gap >= 1:
            fresh = []
            for k in range(len(keys)):
                if gap >= 64:
                    other = lane_take(keys[k], lane ^ lane_of[gap])
                elif gap >= 8:
                    other = keys[k ^ (gap // 8)]
                else:
                    down = pltpu.roll(keys[k], gap, 0)
                    up = down if gap == 4 else pltpu.roll(keys[k], 8 - gap, 0)
                    other = up if gap == 4 else jnp.where(sub & gap == 0, up, down)
                rising = bit(size, k)
                keep = same(bit(gap, k), True if rising is None else rising)
                if isinstance(keep, bool):
                    fresh.append(jnp.minimum(keys[k], other) if keep else jnp.maximum(keys[k], other))
                else:
                    fresh.append(jnp.where(keep, jnp.minimum(keys[k], other), jnp.maximum(keys[k], other)))
            keys = fresh
            gap //= 2
        size *= 2
    return keys


def upright(rows):
    half = rows.T
    joined = jnp.concatenate([half[0:64], half[64:128]], axis=1)
    return [joined[8 * k : 8 * k + 8] for k in range(8)]


def flat(blocks):
    joined = jnp.concatenate(blocks, axis=0)
    return jnp.concatenate([joined[:, 0:64], joined[:, 64:128]], axis=0).T


def remainder(key):
    return key - jnp.floor(key * (1.0 / CELL)) * CELL


def order_kernel(core_ref, out_ref, back_ref, tail_ref, head_ref, spare):
    lane = lax.broadcasted_iota(jnp.int32, (CPD, LANES), 1)
    x = [by_group(core_ref, 0, g) for g in range(GROUPS)]
    low = jnp.min(jnp.minimum(jnp.minimum(x[0], x[1]), jnp.minimum(x[2], x[3])), axis=1, keepdims=True)
    high = jnp.max(jnp.maximum(jnp.maximum(x[0], x[1]), jnp.maximum(x[2], x[3])), axis=1, keepdims=True)
    scale = (BINS - 1.0) / jnp.maximum(high - low, tiny)
    for g in range(GROUPS):
        bin_at = jnp.floor((x[g] - low) * scale)
        bin_at = jnp.where(bin_at > 0.0, jnp.minimum(bin_at, BINS - 1.0), 0.0)
        spare[pl.ds(g, CPD, stride=GROUPS), :] = bin_at * CELL + (lane + g * LANES).astype(jnp.float32)
    keys = ordered(upright(spare[...]))
    source = [remainder(k) for k in keys]
    spare[...] = flat(source)
    wide = lax.broadcasted_iota(jnp.int32, (8, LANES), 1)
    deep = lax.broadcasted_iota(jnp.int32, (8, LANES), 0)
    above = (wide & 3) * LANES + (wide >> 6) * 64 + deep
    places = [(above + 8 * k).astype(jnp.float32) for k in range(8)]
    back = ordered([s * CELL + p for s, p in zip(source, places)])
    back_ref[...] = flat([remainder(k) for k in back]).astype(jnp.int32)
    whole = [spare[pl.ds(g, CPD, stride=GROUPS), :].astype(jnp.int32) for g in range(GROUPS)]
    for f, plane in enumerate((0, 1, 2, 4, 3)):
        had = [by_group(core_ref, plane, g) for g in range(GROUPS)]
        if plane == 4:
            had = [0.5 * h for h in had]
        now = []
        for g in range(GROUPS):
            group_at, lane_at = whole[g] >> 7, whole[g] & (LANES - 1)
            value = lane_take(had[0], lane_at)
            for other in range(1, GROUPS):
                value = jnp.where(group_at == other, lane_take(had[other], lane_at), value)
            now.append(value)
            out_ref[f, pl.ds(g, CPD, stride=GROUPS), :] = value
        if plane == 0:
            lows = [jnp.min(v, axis=1, keepdims=True) for v in now]
            highs = [jnp.max(v, axis=1, keepdims=True) for v in now]
        if plane == 4:
            tops = jnp.max(jnp.maximum(jnp.maximum(now[0], now[1]), jnp.maximum(now[2], now[3])), axis=1, keepdims=True)
    for g in range(GROUPS):
        stat = jnp.where(lane == 0, lows[g], jnp.where(lane == 1, highs[g], tops))
        out_ref[5, pl.ds(g, CPD, stride=GROUPS), :] = stat
    tail_ref[...] = out_ref[:, ROWS - REACH : ROWS, :]
    head_ref[...] = out_ref[:, 0:REACH, :]


def order(core):
    return pl.pallas_call(
        order_kernel,
        out_shape=(
            jax.ShapeDtypeStruct((6, ROWS, LANES), jnp.float32),
            jax.ShapeDtypeStruct((ROWS, LANES), jnp.int32),
            jax.ShapeDtypeStruct((6, REACH, LANES), jnp.float32),
            jax.ShapeDtypeStruct((6, REACH, LANES), jnp.float32),
        ),
        in_specs=[vmem()],
        out_specs=(vmem(),) * 4,
        scratch_shapes=[pltpu.VMEM((ROWS, LANES), jnp.float32)],
        cost_estimate=pl.CostEstimate(flops=3000000, bytes_accessed=400000, transcendentals=0),
compiler_params=pltpu.CompilerParams(vmem_limit_bytes=GRANT),
        name="order",
    )(core)


def own_kernel(z_length, stat_ref, core_ref, out_ref, cols, mirror):
    low, high = span(core_ref[2])
    plain = high - low <= 0.5 * z_length

    @pl.when(plain)
    def _():
        @pl.loop(0, CPD)
        def _(cell):
            fields = load_cell(core_ref, cell)
            fill_cols(cols, fields)
            rows = spread_rows(fields)
            put_total(out_ref, cell, mirror_block(cols, rows, mirror), False)
            run_corners(out_ref, cell, cols, rows, far_groups(stat_ref, cell, stat_ref, cell))

    @pl.when(jnp.logical_not(plain))
    def _():
        @pl.loop(0, CPD)
        def _(cell):
            fields = load_cell(core_ref, cell)
            fill_cols(cols, fields)
            put_total(out_ref, cell, dense_block(cols, spread_rows(fields), z_length), False)


def stat_spec(rows=ROWS):
    return pl.BlockSpec((1, rows, LANES), lambda i: (5, 0, 0), memory_space=pltpu.SMEM)


def own_density(core, z_length):
    return pl.pallas_call(
        functools.partial(own_kernel, z_length),
        out_shape=jax.ShapeDtypeStruct((ROWS, LANES), jnp.float32),
        in_specs=[stat_spec(), vmem()],
        out_specs=vmem(),
        scratch_shapes=[pltpu.VMEM((5, CELL, LANES), jnp.float32), pltpu.VMEM((CELL, LANES), jnp.float32)],
        cost_estimate=pl.CostEstimate(flops=CPD * CELL * CELL * 12, bytes_accessed=400000, transcendentals=0),
        grid=(1,),
compiler_params=pltpu.CompilerParams(vmem_limit_bytes=GRANT),
        name="own_density",
    )(core, core)


def lane_take(values, lanes):
    return jnp.take_along_axis(values, lanes, axis=1, mode="promise_in_bounds")


def hole_rates(sums, hole_vel, hole_mass):
    mass_sum = sums[0]
    mean_heat = sums[1] / mass_sum
    drift = [v - s / mass_sum for v, s in zip(hole_vel, sums[2:5])]
    speed_sq = heat_coef * mean_heat + (drift[0] * drift[0] + drift[1] * drift[1] + drift[2] * drift[2])
    rho_hole = mass_sum / sums[5]
    bondi = bondi_coef * hole_mass * hole_mass * rho_hole / (speed_sq * jnp.sqrt(speed_sq))
    limit = edd_coef * hole_mass
    rate = jnp.minimum(bondi, limit)
    return rate, rate / limit, rho_hole


def pairs_kernel(
    z_length,
    pairs_ref,
    stat_ref,
    lower_stat_ref,
    upper_stat_ref,
    sorted_ref,
    lower_ref,
    upper_ref,
    own_ref,
    back_ref,
    core_ref,
    vel_ref,
    energy_ref,
    gas_id_ref,
    slot_ref,
    rho_ref,
    picked_ref,
    place_ref,
    cells,
    cols,
    held_rho,
):
    blocks = CAP // 8
    lane = lax.broadcasted_iota(jnp.int32, (8, LANES), 1)
    sub = lax.broadcasted_iota(jnp.int32, (8, LANES), 0)
    coded = gas_id_ref[...] * LANES + slot_ref[...]
    for v in range(blocks):
        place = CAP * lane + (8 * v + sub)
        place_row, place_lane = place >> 7, place & (LANES - 1)
        piece = jnp.zeros((8, LANES), jnp.int32)
        for r in range(CAP):
            row = jnp.broadcast_to(coded[r : r + 1], (8, LANES))
            piece = jnp.where(place_row == r, lane_take(row, place_lane), piece)
        place_ref[8 * v : 8 * v + 8, :] = piece
    sources = [(core_ref, 0), (core_ref, 1), (core_ref, 2)] + [(vel_ref, 0), (vel_ref, 1), (vel_ref, 2)]
    sources = sources + [(core_ref, 3), (energy_ref, 0)]
    per_step = ROWS // NPAIR

    def pick(first, lines):
        for v in range(blocks):
            part = slice(8 * v, 8 * v + 8)
            at = place_ref[part, :]
            gas_row, gas_lane = at >> 14, (at >> 7) & (LANES - 1)
            here = [gas_row == first + inner for inner in range(per_step)]
            for field, (ref, plane) in lines:
                value = picked_ref[field, part, :]
                for inner in range(per_step):
                    line = ref[pl.ds(first + inner, 1), :] if plane is None else ref[plane, pl.ds(first + inner, 1), :]
                    moved = lane_take(jnp.broadcast_to(line, (8, LANES)), gas_lane)
                    value = jnp.where(here[inner], moved, value)
                picked_ref[field, part, :] = value

    def pick_rows(step):
        pick(step * per_step, list(enumerate(sources)))

    half = 0.5 * z_length
    low, high = span(sorted_ref[2])
    plain = high - low <= half
    edges = ((lower_ref, slice(0, REACH), 0), (upper_ref, slice(0, REACH), REACH + ROWS))
    for ref, part, at in edges:
        z = ref[2, part, :]
        edge_low, edge_high = span(z)
        above = edge_low - high > half
        below = low - edge_high > half
        inside = jnp.logical_and(edge_high - low <= half, high - edge_low <= half)
        plain = jnp.logical_and(plain, jnp.logical_or(inside, jnp.logical_or(above, below)))
        shift = jnp.where(above, -z_length, jnp.where(below, z_length, 0.0))
        for f in (0, 1, 3, 4):
            cells[f, at : at + REACH, :] = ref[f, part, :]
        cells[2, at : at + REACH, :] = z + shift
    for f in range(5):
        cells[f, REACH : REACH + ROWS, :] = sorted_ref[f]
    held_rho[...] = own_ref[...]

    @pl.when(plain)
    def _():
        @pl.loop(0, NPAIR)
        def _(step):
            home = pairs_ref[0, step]
            other = pairs_ref[1, step]
            fill_cols(cols, load_cell(cells, other))
            rows = spread_rows(load_cell(sorted_ref, home))
            pick_rows(step)
            put_total(held_rho, home, band_block(cols, rows), True)

            def corners(q_stat, q_cell):
                run_corners(held_rho, home, cols, rows, far_groups(stat_ref, home, q_stat, q_cell))

            pl.when(other < BND)(lambda: corners(lower_stat_ref, other))
            pl.when(other >= BND + CPD)(lambda: corners(upper_stat_ref, other - (BND + CPD)))
            pl.when(jnp.logical_and(other >= BND, other < BND + CPD))(lambda: corners(stat_ref, other - BND))

    @pl.when(jnp.logical_not(plain))
    def _():
        for ref, part, at in edges:
            cells[2, at : at + REACH, :] = ref[2, part, :]

        @pl.loop(0, NPAIR)
        def _(step):
            home = pairs_ref[0, step]
            fill_cols(cols, load_cell(cells, pairs_ref[1, step]))
            pick_rows(step)
            rows = spread_rows(load_cell(sorted_ref, home))
            put_total(held_rho, home, dense_block(cols, rows, z_length), True)

    for g in range(GROUPS):
        back = back_ref[pl.ds(g, CPD, stride=GROUPS), :]
        group_at, lane_at = back >> 7, back & (LANES - 1)
        value = lane_take(held_rho[pl.ds(0, CPD, stride=GROUPS), :], lane_at)
        for other in range(1, GROUPS):
            moved = lane_take(held_rho[pl.ds(other, CPD, stride=GROUPS), :], lane_at)
            value = jnp.where(group_at == other, moved, value)
        rho_ref[pl.ds(g, CPD, stride=GROUPS), :] = value

    for step in range(NPAIR):
        pick(step * per_step, [(STATIC, (rho_ref, None))])


def pairs_density(pairs, ranked, lower, upper, own, back, core, vel, energy, gas_id, slot, z_length):
    smem = pl.BlockSpec(memory_space=pltpu.SMEM)
    return pl.pallas_call(
        functools.partial(pairs_kernel, z_length),
        out_shape=(
            jax.ShapeDtypeStruct((ROWS, LANES), jnp.float32),
            jax.ShapeDtypeStruct((STATIC + 1, CAP, LANES), jnp.float32),
            jax.ShapeDtypeStruct((CAP, LANES), jnp.int32),
        ),
        in_specs=[smem, stat_spec(), stat_spec(REACH), stat_spec(REACH)] + [vmem()] * 10,
        out_specs=(vmem(),) * 3,
        scratch_shapes=[
            pltpu.VMEM((5, 2 * REACH + ROWS, LANES), jnp.float32),
            pltpu.VMEM((5, CELL, LANES), jnp.float32),
            pltpu.VMEM((ROWS, LANES), jnp.float32),
        ],
        cost_estimate=pl.CostEstimate(flops=NPAIR * CELL * CELL * 17, bytes_accessed=2000000, transcendentals=0),
        grid=(1,),
compiler_params=pltpu.CompilerParams(vmem_limit_bytes=GRANT),
        name="pairs_density",
    )(pairs, ranked, lower, upper, ranked, lower, upper, own, back, core, vel, energy, gas_id, slot)


def feed_kernel(y_length, z_length, group, picked_ref, place_ref, count_ref, holes_ref, message_ref, lost_ref, gas_at_ref):
    gas = [picked_ref[f] for f in range(STATIC + 1)]
    place = place_ref[...]
    slot = place & (LANES - 1)
    count = count_ref[...]
    live = lax.broadcasted_iota(jnp.int32, (CAP, LANES), 0) < count

    first = slot[0:1]
    second = jnp.max(jnp.where(live & (slot != first), slot, -1), axis=0, keepdims=True)
    is_first = live & (slot == first)
    is_second = live & (slot != first)

    two = jnp.concatenate([first, jnp.maximum(second, 0)] * (LANES // 2), axis=0)
    chosen = two.astype(jnp.float32).T.astype(jnp.int32)
    wide_lane = lax.broadcasted_iota(jnp.int32, (LANES, LANES), 1)
    held = jnp.zeros((LANES, LANES), jnp.float32)
    for f in range(8):
        table = holes_ref[pl.ds(f, group, stride=8), :]
        held = jnp.where((wide_lane >> 1) == f, lane_take(table, chosen), held)
    held = held.T
    hole_first = [held[2 * f : 2 * f + 1] for f in range(8)]
    hole_second = [held[2 * f + 1 : 2 * f + 2] for f in range(8)]
    hole = [jnp.where(is_first, a, b) for a, b in zip(hole_first, hole_second)]

    delta_x = gas[0] - hole[0]
    delta_y = nearest(gas[1] - hole[1], y_length)
    delta_z = nearest(gas[2] - hole[2], z_length)
    spread_sq = (delta_x * delta_x + delta_y * delta_y + delta_z * delta_z) / (hole[7] * hole[7])
    soft = 1.0 / (1.0 + spread_sq)
    weight = jnp.where(live, soft * soft, 0.0)
    mass_w = gas[6] * weight
    volume = mass_w / jnp.where(live, gas[8], 1.0)
    terms = [mass_w, mass_w * gas[7], mass_w * gas[3], mass_w * gas[4], mass_w * gas[5], volume]

    def settle(mine, held_by):
        sums = [jnp.sum(jnp.where(mine, t, 0.0), axis=0, keepdims=True) for t in terms]
        rate, ratio, rho_hole = hole_rates(sums, held_by[3:6], held_by[6])
        return step_dt * rate, sums[5], ratio, rho_hole

    gain_a, volume_a, ratio_a, rho_a = settle(is_first, hole_first)
    gain_b, volume_b, ratio_b, rho_b = settle(is_second, hole_second)
    lost = jnp.where(is_first, gain_a, gain_b) * (volume / jnp.where(is_first, volume_a, volume_b))
    lost = jnp.where(live, lost, 0.0)

    has_a = count > 0
    has_b = second >= 0
    lines = [
        jnp.where(has_a, first.astype(jnp.float32), -1.0),
        jnp.where(has_a, ratio_a, 0.0),
        jnp.where(has_a, rho_a, 0.0),
        second.astype(jnp.float32),
        jnp.where(has_b, ratio_b, 0.0),
        jnp.where(has_b, rho_b, 0.0),
        jnp.zeros((2, LANES), jnp.float32),
    ]
    lines = jnp.concatenate(lines + [jnp.zeros((LANES - 8, LANES), jnp.float32)], axis=0)
    message_ref[...] = lines.T[:, 0:8]
    lost_ref[...] = lost
    gas_at_ref[...] = place >> 7


def feed(picked, place, count, holes, y_length, z_length, group):
    return pl.pallas_call(
        functools.partial(feed_kernel, y_length, z_length, group),
        out_shape=(
            jax.ShapeDtypeStruct((group, 8), jnp.float32),
            jax.ShapeDtypeStruct((CAP, LANES), jnp.float32),
            jax.ShapeDtypeStruct((CAP, LANES), jnp.int32),
        ),
        in_specs=[vmem()] * 4,
        out_specs=(vmem(),) * 3,
        cost_estimate=pl.CostEstimate(flops=1000000, bytes_accessed=1000000, transcendentals=0),
compiler_params=pltpu.CompilerParams(vmem_limit_bytes=GRANT),
        name="feed",
    )(picked, place, count, holes)


def apply_kernel(lost_ref, gas_at_ref, core_ref, energy_ref, update_ref):
    lost = lost_ref[...]
    gas_row, gas_lane = gas_at_ref[...] >> 7, gas_at_ref[...] & (LANES - 1)
    high = lost.astype(jnp.bfloat16).astype(jnp.float32)
    mid = (lost - high).astype(jnp.bfloat16).astype(jnp.float32)
    low = (lost - high) - mid
    tall = lax.broadcasted_iota(jnp.int32, (LANES, LANES), 0)
    total = jnp.zeros((ROWS, 3 * LANES), jnp.float32)
    for k in range(CAP):
        at_row = (tall[:ROWS] == gas_row[k : k + 1]).astype(jnp.float32).astype(jnp.bfloat16)
        at_lane = tall == gas_lane[k : k + 1]
        parts = [jnp.where(at_lane, part[k : k + 1], 0.0).astype(jnp.bfloat16) for part in (high, mid, low)]
        total = total + lax.dot_general(
            at_row,
            jnp.concatenate(parts, axis=0),
            (((1,), (1,)), ((), ())),
            preferred_element_type=jnp.float32,
        )
    taken = total[:, 0:LANES] + total[:, LANES : 2 * LANES] + total[:, 2 * LANES :]
    mass = core_ref[0]
    update_ref[0] = mass - taken
    update_ref[1] = energy_ref[...] + feed_coef * taken / mass


def apply(lost, gas_at, core, energy):
    mass_spec = pl.BlockSpec((1, ROWS, LANES), lambda i: (3, 0, 0), memory_space=pltpu.VMEM)
    return pl.pallas_call(
        apply_kernel,
        out_shape=jax.ShapeDtypeStruct((2, ROWS, LANES), jnp.float32),
        in_specs=[vmem(), vmem(), mass_spec, vmem()],
        out_specs=vmem(),
        cost_estimate=pl.CostEstimate(flops=1000000, bytes_accessed=100000, transcendentals=0),
        grid=(1,),
compiler_params=pltpu.CompilerParams(vmem_limit_bytes=GRANT),
        name="apply",
    )(lost, gas_at, core, energy)


def spread_kernel(group, coord_ref, vel_ref, mass_ref, soft_ref, pairs_ref, count_ref, out_ref, pairs_out, count_out):
    pairs_out[...] = pairs_ref[...]
    count_out[...] = count_ref[...]
    lines = [coord_ref[f] for f in range(3)] + [vel_ref[f] for f in range(3)] + [mass_ref[0], soft_ref[0]]
    out_ref[...] = jnp.broadcast_to(jnp.concatenate(lines, axis=0)[None], (group, 8, LANES))


def spread(coord, vel, mass, soft, pairs, count, group):
    return pl.pallas_call(
        functools.partial(spread_kernel, group),
        out_shape=(
            jax.ShapeDtypeStruct((group, 8, LANES), jnp.float32),
            jax.ShapeDtypeStruct((2, NPAIR), jnp.int32),
            jax.ShapeDtypeStruct((1, LANES), jnp.int32),
        ),
        in_specs=[vmem()] * 6,
        out_specs=(vmem(),) * 3,
        compiler_params=pltpu.CompilerParams(vmem_limit_bytes=GRANT),
        name="spread",
    )(coord, vel, mass, soft, pairs, count)


def settle_kernel(group, arrived_ref, out_ref):
    lane = lax.broadcasted_iota(jnp.int32, (group, LANES), 1).astype(jnp.float32)
    parts = [jnp.broadcast_to(arrived_ref[:, f : f + 1], (group, LANES)) for f in range(6)]
    at_first = lane == parts[0]
    at_second = lane == parts[3]
    for k in range(2):
        value = jnp.where(at_first, parts[1 + k], jnp.where(at_second, parts[4 + k], 0.0))
        out_ref[k] = jnp.sum(value, axis=0, keepdims=True)


def settle(arrived, group):
    return pl.pallas_call(
        functools.partial(settle_kernel, group),
        out_shape=jax.ShapeDtypeStruct((2, 1, LANES), jnp.float32),
        in_specs=[vmem()],
        out_specs=vmem(),
compiler_params=pltpu.CompilerParams(vmem_limit_bytes=GRANT),
        name="settle",
    )(arrived)


def body(gas_core, gas_vel, gas_energy, cell_pairs, bh_coord, bh_vel, bh_mass, bh_soft, mem_gas, mem_slot, send_count):
    group = lax.axis_size("dy") * lax.axis_size("dz")
    deep = lax.axis_size("dz")
    z_length = cell_height * CPD * deep
    y_length = face_width * lax.axis_size("dy")
    core = gas_core.reshape(5, ROWS, LANES)
    energy = gas_energy.reshape(ROWS, LANES)
    ranked, back, tail, head = order(core)
    lower = lax.ppermute(tail, "dz", [(i, (i + 1) % deep) for i in range(deep)])
    upper = lax.ppermute(head, "dz", [((i + 1) % deep, i) for i in range(deep)])
    copies, pairs, count = spread(
        bh_coord.reshape(3, 1, LANES),
        bh_vel.reshape(3, 1, LANES),
        bh_mass.reshape(1, 1, LANES),
        bh_soft.reshape(1, 1, LANES),
        cell_pairs.reshape(2, NPAIR),
        send_count.reshape(1, LANES),
        group,
    )
    holes = lax.all_to_all(copies, ("dy", "dz"), split_axis=0, concat_axis=0, tiled=True).reshape(group * 8, LANES)
    own = own_density(ranked, z_length)
    rho, picked, place = pairs_density(
        pairs,
        ranked,
        lower,
        upper,
        own,
        back,
        core,
        gas_vel.reshape(3, ROWS, LANES),
        energy.reshape(1, ROWS, LANES),
        mem_gas.reshape(CAP, LANES),
        mem_slot.reshape(CAP, LANES),
        z_length,
    )
    message, lost, gas_at = feed(picked, place, count, holes, y_length, z_length, group)
    arrived = lax.all_to_all(message, ("dy", "dz"), split_axis=0, concat_axis=0, tiled=True)
    update = apply(lost, gas_at, core, energy)
    bh_update = settle(arrived, group)
    return (
        rho.reshape(1, 1, CPD * CELL),
        update.reshape(2, 1, 1, CPD * CELL),
        bh_update.reshape(2, 1, 1, LANES),
    )


def solution(mesh):
    lead, plain = P(None, "dx", "dy", "dz"), P("dx", "dy", "dz")
    in_specs = (lead, lead, plain, lead, lead, lead, plain, plain, plain, plain, plain)
    return jax.shard_map(body, mesh=mesh, in_specs=in_specs, out_specs=(plain, lead, lead), check_vma=False)
```

```python
import functools
import math

import jax
import jax.numpy as jnp
from jax import lax
from jax.experimental import pallas as pl
from jax.experimental.pallas import tpu as pltpu
from jax.sharding import PartitionSpec as P

CELL = 512
CPD = 16
BND = 10
NPAIR = 16
CAP = 24
LANES = 128
GROUPS = CELL // LANES
ROWS = CPD * GROUPS
REACH = BND * GROUPS
TILES = LANES // 8
BINS = 32768.0
UNROLL = 16
STATIC = 8
GRANT = 16 * 1024 * 1024

kernel_norm = 21.0 / (2.0 * math.pi)
face_width = 32.0
cell_height = 0.5
bondi_coef = 0.04
edd_coef = 0.25
step_dt = 0.05
feed_coef = 20.0
heat_coef = 10.0 / 9.0
tiny = 1e-37


def vmem():
    return pl.BlockSpec(memory_space=pltpu.VMEM)


def nearest(delta, length):
    half = 0.5 * length
    return jnp.where(delta > half, delta - length, jnp.where(delta < -half, delta + length, delta))


def pair_term(p, q, wrap):
    dx = p[0] - q[0]
    dy = p[1] - q[1]
    dz = p[2] - q[2]
    if wrap is not None:
        dz = jnp.abs(dz)
        dz = jnp.minimum(dz, wrap - dz)
    dist_sq = jnp.maximum(dx * dx + dy * dy + dz * dz, tiny)
    smooth = p[3] + q[3]
    inverse = lax.rsqrt(smooth * smooth)
    rest = jnp.maximum(1.0 - (dist_sq * lax.rsqrt(dist_sq)) * inverse, 0.0)
    scaled = rest * inverse
    return (scaled * scaled) * (scaled * (rest * (1.25 - rest)))


def load_cols(cols, tile):
    return [cols[f, pl.ds(pl.multiple_of(tile * 8, 8), 8), :] for f in range(5)]


def fold(parts):
    return jnp.sum(parts, axis=0, keepdims=True)


def dense_block(cols, rows, wrap):
    def step(turn, total):
        total = list(total)
        for inner in range(4):
            q = load_cols(cols, turn * 4 + inner)
            for g in range(GROUPS):
                total[g] = total[g] + pair_term(rows[g], q, wrap) * q[4]
        return tuple(total)

    zero = jnp.zeros((8, LANES), jnp.float32)
    return lax.fori_loop(0, CELL // 32, step, (zero,) * GROUPS)


def band_block(cols, rows):
    def step(turn, total):
        total = list(total)
        for h in range(GROUPS):
            for inner in range(UNROLL):
                q = load_cols(cols, h * TILES + turn * UNROLL + inner)
                for g in range(max(h - 1, 0), min(h + 2, GROUPS)):
                    total[g] = total[g] + pair_term(rows[g], q, None) * q[4]
        return tuple(total)

    zero = jnp.zeros((8, LANES), jnp.float32)
    return lax.fori_loop(0, TILES // UNROLL, step, (zero,) * GROUPS)


def mirror_block(cols, rows, mirror):
    def step(turn, total):
        total = list(total)
        for h in range(GROUPS):
            for inner in range(UNROLL):
                tile = turn * UNROLL + inner
                q = load_cols(cols, h * TILES + tile)
                total[h] = total[h] + pair_term(rows[h], q, None) * q[4]
                if h + 1 < GROUPS:
                    term = pair_term(rows[h + 1], q, None)
                    total[h + 1] = total[h + 1] + term * q[4]
                    mirror[pl.ds(pl.multiple_of((h * TILES + tile) * 8, 8), 8), :] = term * rows[h + 1][4]
        return tuple(total)

    zero = jnp.zeros((8, LANES), jnp.float32)
    total = list(lax.fori_loop(0, TILES // UNROLL, step, (zero,) * GROUPS))
    for h in range(GROUPS - 1):
        part = mirror[h * LANES : (h + 1) * LANES, :].T
        total[h] = total[h] + jnp.sum(part.reshape(TILES, 8, LANES), axis=0)
    return total


def corner_block(cols, row, h):
    def step(turn, total):
        for inner in range(4):
            q = load_cols(cols, h * TILES + turn * 4 + inner)
            total = total + pair_term(row, q, None) * q[4]
        return total

    return lax.fori_loop(0, TILES // 4, step, jnp.zeros((8, LANES), jnp.float32))


def cell_rows(cell):
    return pl.ds(pl.multiple_of(cell * GROUPS, GROUPS), GROUPS)


def load_cell(ref, cell):
    return [ref[f, cell_rows(cell), :] for f in range(5)]


def fill_cols(cols, fields):
    for g in range(GROUPS):
        for f in range(5):
            cols[f, g * LANES : (g + 1) * LANES, :] = jnp.broadcast_to(fields[f][g : g + 1], (LANES, LANES)).T


def spread_rows(fields):
    return [[jnp.broadcast_to(f[g : g + 1], (8, LANES)) for f in fields] for g in range(GROUPS)]


def put_total(out_ref, cell, total, add):
    summed = jnp.concatenate([fold(t) for t in total], axis=0) * (4.0 * kernel_norm)
    out_ref[cell_rows(cell), :] = out_ref[cell_rows(cell), :] + summed if add else summed


def far_groups(p_stat, p_cell, q_stat, q_cell):
    reach = p_stat[0, 2, p_cell * GROUPS] + q_stat[0, 2, q_cell * GROUPS]
    reach = reach * 1.0001
    found = []
    for g in range(GROUPS):
        for h in range(GROUPS):
            if abs(g - h) >= 2:
                p_low, p_high = p_stat[0, 0, p_cell * GROUPS + g], p_stat[0, 1, p_cell * GROUPS + g]
                q_low, q_high = q_stat[0, 0, q_cell * GROUPS + h], q_stat[0, 1, q_cell * GROUPS + h]
                near = jnp.logical_and(p_low - q_high <= reach, q_low - p_high <= reach)
                found.append((g, h, near))
    return found


def run_corners(out_ref, cell, cols, rows, found):
    some = functools.reduce(jnp.logical_or, [near for _, _, near in found])

    @pl.when(some)
    def _():
        for g, h, near in found:

            @pl.when(near)
            def _():
                part = fold(corner_block(cols, rows[g], h)) * (4.0 * kernel_norm)
                at = pl.ds(cell * GROUPS + g, 1)
                out_ref[at, :] = out_ref[at, :] + part


def span(z):
    return jnp.min(z), jnp.max(z)


def by_group(ref, plane, g):
    return ref[plane, pl.ds(g, CPD, stride=GROUPS), :]


def ordered(keys):
    depth = CELL // 8
    lane = lax.broadcasted_iota(jnp.int32, (8, LANES), 1)
    sub = lax.broadcasted_iota(jnp.int32, (8, LANES), 0)
    lane_of = {64: 64, 128: 1, 256: 2}

    def bit(step, block):
        if step < 8:
            return sub & step == 0
        if step < 64:
            return block * 8 & step == 0
        return None if step >= CELL else lane & lane_of[step] == 0

    def same(a, b):
        if isinstance(a, bool) and isinstance(b, bool):
            return a == b
        if isinstance(a, bool):
            a, b = b, a
        if isinstance(b, bool):
            return a if b else jnp.logical_not(a)
        return jnp.logical_not(jnp.logical_xor(a, b))

    size = 2
    while size <= CELL:
        gap = size // 2
        while gap >= 1:
            fresh = []
            for k in range(len(keys)):
                if gap >= 64:
                    other = lane_take(keys[k], lane ^ lane_of[gap])
                elif gap >= 8:
                    other = keys[k ^ (gap // 8)]
                else:
                    down = pltpu.roll(keys[k], gap, 0)
                    up = down if gap == 4 else pltpu.roll(keys[k], 8 - gap, 0)
                    other = up if gap == 4 else jnp.where(sub & gap == 0, up, down)
                rising = bit(size, k)
                keep = same(bit(gap, k), True if rising is None else rising)
                if isinstance(keep, bool):
                    fresh.append(jnp.minimum(keys[k], other) if keep else jnp.maximum(keys[k], other))
                else:
                    fresh.append(jnp.where(keep, jnp.minimum(keys[k], other), jnp.maximum(keys[k], other)))
            keys = fresh
            gap //= 2
        size *= 2
    return keys


def upright(rows):
    half = rows.T
    joined = jnp.concatenate([half[0:64], half[64:128]], axis=1)
    return [joined[8 * k : 8 * k + 8] for k in range(8)]


def flat(blocks):
    joined = jnp.concatenate(blocks, axis=0)
    return jnp.concatenate([joined[:, 0:64], joined[:, 64:128]], axis=0).T


def remainder(key):
    return key - jnp.floor(key * (1.0 / CELL)) * CELL


def order_kernel(core_ref, out_ref, back_ref, tail_ref, head_ref, spare):
    lane = lax.broadcasted_iota(jnp.int32, (CPD, LANES), 1)
    x = [by_group(core_ref, 0, g) for g in range(GROUPS)]
    low = jnp.min(jnp.minimum(jnp.minimum(x[0], x[1]), jnp.minimum(x[2], x[3])), axis=1, keepdims=True)
    high = jnp.max(jnp.maximum(jnp.maximum(x[0], x[1]), jnp.maximum(x[2], x[3])), axis=1, keepdims=True)
    scale = (BINS - 1.0) / jnp.maximum(high - low, tiny)
    for g in range(GROUPS):
        bin_at = jnp.floor((x[g] - low) * scale)
        bin_at = jnp.where(bin_at > 0.0, jnp.minimum(bin_at, BINS - 1.0), 0.0)
        spare[pl.ds(g, CPD, stride=GROUPS), :] = bin_at * CELL + (lane + g * LANES).astype(jnp.float32)
    keys = ordered(upright(spare[...]))
    source = [remainder(k) for k in keys]
    spare[...] = flat(source)
    wide = lax.broadcasted_iota(jnp.int32, (8, LANES), 1)
    deep = lax.broadcasted_iota(jnp.int32, (8, LANES), 0)
    above = (wide & 3) * LANES + (wide >> 6) * 64 + deep
    places = [(above + 8 * k).astype(jnp.float32) for k in range(8)]
    back = ordered([s * CELL + p for s, p in zip(source, places)])
    back_ref[...] = flat([remainder(k) for k in back]).astype(jnp.int32)
    whole = [spare[pl.ds(g, CPD, stride=GROUPS), :].astype(jnp.int32) for g in range(GROUPS)]
    for f, plane in enumerate((0, 1, 2, 4, 3)):
        had = [by_group(core_ref, plane, g) for g in range(GROUPS)]
        if plane == 4:
            had = [0.5 * h for h in had]
        now = []
        for g in range(GROUPS):
            group_at, lane_at = whole[g] >> 7, whole[g] & (LANES - 1)
            value = lane_take(had[0], lane_at)
            for other in range(1, GROUPS):
                value = jnp.where(group_at == other, lane_take(had[other], lane_at), value)
            now.append(value)
            out_ref[f, pl.ds(g, CPD, stride=GROUPS), :] = value
        if plane == 0:
            lows = [jnp.min(v, axis=1, keepdims=True) for v in now]
            highs = [jnp.max(v, axis=1, keepdims=True) for v in now]
        if plane == 4:
            tops = jnp.max(jnp.maximum(jnp.maximum(now[0], now[1]), jnp.maximum(now[2], now[3])), axis=1, keepdims=True)
    for g in range(GROUPS):
        stat = jnp.where(lane == 0, lows[g], jnp.where(lane == 1, highs[g], tops))
        out_ref[5, pl.ds(g, CPD, stride=GROUPS), :] = stat
    tail_ref[...] = out_ref[:, ROWS - REACH : ROWS, :]
    head_ref[...] = out_ref[:, 0:REACH, :]
    turned = out_ref[5].T[0:8]
    turned = jnp.concatenate([turned, turned], axis=1)
    for ref in (out_ref, tail_ref, head_ref):
        ref[5, 0:8, :] = turned


def order(core):
    return pl.pallas_call(
        order_kernel,
        out_shape=(
            jax.ShapeDtypeStruct((6, ROWS, LANES), jnp.float32),
            jax.ShapeDtypeStruct((ROWS, LANES), jnp.int32),
            jax.ShapeDtypeStruct((6, REACH, LANES), jnp.float32),
            jax.ShapeDtypeStruct((6, REACH, LANES), jnp.float32),
        ),
        in_specs=[vmem()],
        out_specs=(vmem(),) * 4,
        scratch_shapes=[pltpu.VMEM((ROWS, LANES), jnp.float32)],
        cost_estimate=pl.CostEstimate(flops=3000000, bytes_accessed=400000, transcendentals=0),
compiler_params=pltpu.CompilerParams(vmem_limit_bytes=GRANT),
        name="order",
    )(core)


def own_kernel(z_length, stat_ref, core_ref, out_ref, cols, mirror):
    low, high = span(core_ref[2])
    plain = high - low <= 0.5 * z_length

    @pl.when(plain)
    def _():
        @pl.loop(0, CPD)
        def _(cell):
            fields = load_cell(core_ref, cell)
            fill_cols(cols, fields)
            rows = spread_rows(fields)
            put_total(out_ref, cell, mirror_block(cols, rows, mirror), False)
            run_corners(out_ref, cell, cols, rows, far_groups(stat_ref, cell, stat_ref, cell))

    @pl.when(jnp.logical_not(plain))
    def _():
        @pl.loop(0, CPD)
        def _(cell):
            fields = load_cell(core_ref, cell)
            fill_cols(cols, fields)
            put_total(out_ref, cell, dense_block(cols, spread_rows(fields), z_length), False)


def stat_spec():
    return pl.BlockSpec((1, 8, LANES), lambda i: (5, 0, 0), memory_space=pltpu.SMEM)


def own_density(core, z_length):
    return pl.pallas_call(
        functools.partial(own_kernel, z_length),
        out_shape=jax.ShapeDtypeStruct((ROWS, LANES), jnp.float32),
        in_specs=[stat_spec(), vmem()],
        out_specs=vmem(),
        scratch_shapes=[pltpu.VMEM((5, CELL, LANES), jnp.float32), pltpu.VMEM((CELL, LANES), jnp.float32)],
        cost_estimate=pl.CostEstimate(flops=CPD * CELL * CELL * 12, bytes_accessed=400000, transcendentals=0),
        grid=(1,),
compiler_params=pltpu.CompilerParams(vmem_limit_bytes=GRANT),
        name="own_density",
    )(core, core)


def lane_take(values, lanes):
    return jnp.take_along_axis(values, lanes, axis=1, mode="promise_in_bounds")


def hole_rates(sums, hole_vel, hole_mass):
    mass_sum = sums[0]
    mean_heat = sums[1] / mass_sum
    drift = [v - s / mass_sum for v, s in zip(hole_vel, sums[2:5])]
    speed_sq = heat_coef * mean_heat + (drift[0] * drift[0] + drift[1] * drift[1] + drift[2] * drift[2])
    rho_hole = mass_sum / sums[5]
    bondi = bondi_coef * hole_mass * hole_mass * rho_hole / (speed_sq * jnp.sqrt(speed_sq))
    limit = edd_coef * hole_mass
    rate = jnp.minimum(bondi, limit)
    return rate, rate / limit, rho_hole


def pairs_kernel(
    z_length,
    pairs_ref,
    stat_ref,
    lower_stat_ref,
    upper_stat_ref,
    sorted_ref,
    lower_ref,
    upper_ref,
    own_ref,
    back_ref,
    core_ref,
    vel_ref,
    energy_ref,
    gas_id_ref,
    slot_ref,
    rho_ref,
    picked_ref,
    place_ref,
    cells,
    cols,
    held_rho,
):
    blocks = CAP // 8
    lane = lax.broadcasted_iota(jnp.int32, (8, LANES), 1)
    sub = lax.broadcasted_iota(jnp.int32, (8, LANES), 0)
    coded = gas_id_ref[...] * LANES + slot_ref[...]
    for v in range(blocks):
        place = CAP * lane + (8 * v + sub)
        place_row, place_lane = place >> 7, place & (LANES - 1)
        piece = jnp.zeros((8, LANES), jnp.int32)
        for r in range(CAP):
            row = jnp.broadcast_to(coded[r : r + 1], (8, LANES))
            piece = jnp.where(place_row == r, lane_take(row, place_lane), piece)
        place_ref[8 * v : 8 * v + 8, :] = piece
    sources = [(core_ref, 0), (core_ref, 1), (core_ref, 2)] + [(vel_ref, 0), (vel_ref, 1), (vel_ref, 2)]
    sources = sources + [(core_ref, 3), (energy_ref, 0)]
    per_step = ROWS // NPAIR

    def pick(first, lines):
        for v in range(blocks):
            part = slice(8 * v, 8 * v + 8)
            at = place_ref[part, :]
            gas_row, gas_lane = at >> 14, (at >> 7) & (LANES - 1)
            here = [gas_row == first + inner for inner in range(per_step)]
            for field, (ref, plane) in lines:
                value = picked_ref[field, part, :]
                for inner in range(per_step):
                    line = ref[pl.ds(first + inner, 1), :] if plane is None else ref[plane, pl.ds(first + inner, 1), :]
                    moved = lane_take(jnp.broadcast_to(line, (8, LANES)), gas_lane)
                    value = jnp.where(here[inner], moved, value)
                picked_ref[field, part, :] = value

    def pick_rows(step):
        pick(step * per_step, list(enumerate(sources)))

    half = 0.5 * z_length
    low, high = span(sorted_ref[2])
    plain = high - low <= half
    edges = ((lower_ref, slice(0, REACH), 0), (upper_ref, slice(0, REACH), REACH + ROWS))
    for ref, part, at in edges:
        z = ref[2, part, :]
        edge_low, edge_high = span(z)
        above = edge_low - high > half
        below = low - edge_high > half
        inside = jnp.logical_and(edge_high - low <= half, high - edge_low <= half)
        plain = jnp.logical_and(plain, jnp.logical_or(inside, jnp.logical_or(above, below)))
        shift = jnp.where(above, -z_length, jnp.where(below, z_length, 0.0))
        for f in (0, 1, 3, 4):
            cells[f, at : at + REACH, :] = ref[f, part, :]
        cells[2, at : at + REACH, :] = z + shift
    for f in range(5):
        cells[f, REACH : REACH + ROWS, :] = sorted_ref[f]
    held_rho[...] = own_ref[...]

    @pl.when(plain)
    def _():
        @pl.loop(0, NPAIR)
        def _(step):
            home = pairs_ref[0, step]
            other = pairs_ref[1, step]
            fill_cols(cols, load_cell(cells, other))
            rows = spread_rows(load_cell(sorted_ref, home))
            pick_rows(step)
            put_total(held_rho, home, band_block(cols, rows), True)

            def corners(q_stat, q_cell):
                run_corners(held_rho, home, cols, rows, far_groups(stat_ref, home, q_stat, q_cell))

            pl.when(other < BND)(lambda: corners(lower_stat_ref, other + (CPD - BND)))
            pl.when(other >= BND + CPD)(lambda: corners(upper_stat_ref, other - (BND + CPD)))
            pl.when(jnp.logical_and(other >= BND, other < BND + CPD))(lambda: corners(stat_ref, other - BND))

    @pl.when(jnp.logical_not(plain))
    def _():
        for ref, part, at in edges:
            cells[2, at : at + REACH, :] = ref[2, part, :]

        @pl.loop(0, NPAIR)
        def _(step):
            home = pairs_ref[0, step]
            fill_cols(cols, load_cell(cells, pairs_ref[1, step]))
            pick_rows(step)
            rows = spread_rows(load_cell(sorted_ref, home))
            put_total(held_rho, home, dense_block(cols, rows, z_length), True)

    for g in range(GROUPS):
        back = back_ref[pl.ds(g, CPD, stride=GROUPS), :]
        group_at, lane_at = back >> 7, back & (LANES - 1)
        value = lane_take(held_rho[pl.ds(0, CPD, stride=GROUPS), :], lane_at)
        for other in range(1, GROUPS):
            moved = lane_take(held_rho[pl.ds(other, CPD, stride=GROUPS), :], lane_at)
            value = jnp.where(group_at == other, moved, value)
        rho_ref[pl.ds(g, CPD, stride=GROUPS), :] = value

    for step in range(NPAIR):
        pick(step * per_step, [(STATIC, (rho_ref, None))])


def pairs_density(pairs, ranked, lower, upper, own, back, core, vel, energy, gas_id, slot, z_length):
    smem = pl.BlockSpec(memory_space=pltpu.SMEM)
    return pl.pallas_call(
        functools.partial(pairs_kernel, z_length),
        out_shape=(
            jax.ShapeDtypeStruct((ROWS, LANES), jnp.float32),
            jax.ShapeDtypeStruct((STATIC + 1, CAP, LANES), jnp.float32),
            jax.ShapeDtypeStruct((CAP, LANES), jnp.int32),
        ),
        in_specs=[smem] + [stat_spec()] * 3 + [vmem()] * 10,
        out_specs=(vmem(),) * 3,
        scratch_shapes=[
            pltpu.VMEM((5, 2 * REACH + ROWS, LANES), jnp.float32),
            pltpu.VMEM((5, CELL, LANES), jnp.float32),
            pltpu.VMEM((ROWS, LANES), jnp.float32),
        ],
        cost_estimate=pl.CostEstimate(flops=NPAIR * CELL * CELL * 17, bytes_accessed=2000000, transcendentals=0),
        grid=(1,),
compiler_params=pltpu.CompilerParams(vmem_limit_bytes=GRANT),
        name="pairs_density",
    )(pairs, ranked, lower, upper, ranked, lower, upper, own, back, core, vel, energy, gas_id, slot)


def feed_kernel(y_length, z_length, group, picked_ref, place_ref, count_ref, holes_ref, message_ref, lost_ref, gas_at_ref):
    gas = [picked_ref[f] for f in range(STATIC + 1)]
    place = place_ref[...]
    slot = place & (LANES - 1)
    count = count_ref[...]
    live = lax.broadcasted_iota(jnp.int32, (CAP, LANES), 0) < count

    first = slot[0:1]
    second = jnp.max(jnp.where(live & (slot != first), slot, -1), axis=0, keepdims=True)
    is_first = live & (slot == first)
    is_second = live & (slot != first)

    two = jnp.concatenate([first, jnp.maximum(second, 0)] * (LANES // 2), axis=0)
    chosen = two.astype(jnp.float32).T.astype(jnp.int32)
    wide_lane = lax.broadcasted_iota(jnp.int32, (LANES, LANES), 1)
    held = jnp.zeros((LANES, LANES), jnp.float32)
    for f in range(8):
        table = holes_ref[pl.ds(f, group, stride=8), :]
        held = jnp.where((wide_lane >> 1) == f, lane_take(table, chosen), held)
    held = held.T
    hole_first = [held[2 * f : 2 * f + 1] for f in range(8)]
    hole_second = [held[2 * f + 1 : 2 * f + 2] for f in range(8)]
    hole = [jnp.where(is_first, a, b) for a, b in zip(hole_first, hole_second)]

    delta_x = gas[0] - hole[0]
    delta_y = nearest(gas[1] - hole[1], y_length)
    delta_z = nearest(gas[2] - hole[2], z_length)
    spread_sq = (delta_x * delta_x + delta_y * delta_y + delta_z * delta_z) / (hole[7] * hole[7])
    soft = 1.0 / (1.0 + spread_sq)
    weight = jnp.where(live, soft * soft, 0.0)
    mass_w = gas[6] * weight
    volume = mass_w / jnp.where(live, gas[8], 1.0)
    terms = [mass_w, mass_w * gas[7], mass_w * gas[3], mass_w * gas[4], mass_w * gas[5], volume]

    def settle(mine, held_by):
        sums = [jnp.sum(jnp.where(mine, t, 0.0), axis=0, keepdims=True) for t in terms]
        rate, ratio, rho_hole = hole_rates(sums, held_by[3:6], held_by[6])
        return step_dt * rate, sums[5], ratio, rho_hole

    gain_a, volume_a, ratio_a, rho_a = settle(is_first, hole_first)
    gain_b, volume_b, ratio_b, rho_b = settle(is_second, hole_second)
    lost = jnp.where(is_first, gain_a, gain_b) * (volume / jnp.where(is_first, volume_a, volume_b))
    lost = jnp.where(live, lost, 0.0)

    has_a = count > 0
    has_b = second >= 0
    lines = [
        jnp.where(has_a, first.astype(jnp.float32), -1.0),
        jnp.where(has_a, ratio_a, 0.0),
        jnp.where(has_a, rho_a, 0.0),
        second.astype(jnp.float32),
        jnp.where(has_b, ratio_b, 0.0),
        jnp.where(has_b, rho_b, 0.0),
        jnp.zeros((2, LANES), jnp.float32),
    ]
    lines = jnp.concatenate(lines + [jnp.zeros((LANES - 8, LANES), jnp.float32)], axis=0)
    message_ref[...] = lines.T[:, 0:8]
    lost_ref[...] = lost
    gas_at_ref[...] = place >> 7


def feed(picked, place, count, holes, y_length, z_length, group):
    return pl.pallas_call(
        functools.partial(feed_kernel, y_length, z_length, group),
        out_shape=(
            jax.ShapeDtypeStruct((group, 8), jnp.float32),
            jax.ShapeDtypeStruct((CAP, LANES), jnp.float32),
            jax.ShapeDtypeStruct((CAP, LANES), jnp.int32),
        ),
        in_specs=[vmem()] * 4,
        out_specs=(vmem(),) * 3,
        cost_estimate=pl.CostEstimate(flops=1000000, bytes_accessed=1000000, transcendentals=0),
compiler_params=pltpu.CompilerParams(vmem_limit_bytes=GRANT),
        name="feed",
    )(picked, place, count, holes)


def apply_kernel(lost_ref, gas_at_ref, core_ref, energy_ref, update_ref):
    lost = lost_ref[...]
    gas_row, gas_lane = gas_at_ref[...] >> 7, gas_at_ref[...] & (LANES - 1)
    high = lost.astype(jnp.bfloat16).astype(jnp.float32)
    mid = (lost - high).astype(jnp.bfloat16).astype(jnp.float32)
    low = (lost - high) - mid
    tall = lax.broadcasted_iota(jnp.int32, (LANES, LANES), 0)
    total = jnp.zeros((ROWS, 3 * LANES), jnp.float32)
    for k in range(CAP):
        at_row = (tall[:ROWS] == gas_row[k : k + 1]).astype(jnp.float32).astype(jnp.bfloat16)
        at_lane = tall == gas_lane[k : k + 1]
        parts = [jnp.where(at_lane, part[k : k + 1], 0.0).astype(jnp.bfloat16) for part in (high, mid, low)]
        total = total + lax.dot_general(
            at_row,
            jnp.concatenate(parts, axis=0),
            (((1,), (1,)), ((), ())),
            preferred_element_type=jnp.float32,
        )
    taken = total[:, 0:LANES] + total[:, LANES : 2 * LANES] + total[:, 2 * LANES :]
    mass = core_ref[0]
    update_ref[0] = mass - taken
    update_ref[1] = energy_ref[...] + feed_coef * taken / mass


def apply(lost, gas_at, core, energy):
    mass_spec = pl.BlockSpec((1, ROWS, LANES), lambda i: (3, 0, 0), memory_space=pltpu.VMEM)
    return pl.pallas_call(
        apply_kernel,
        out_shape=jax.ShapeDtypeStruct((2, ROWS, LANES), jnp.float32),
        in_specs=[vmem(), vmem(), mass_spec, vmem()],
        out_specs=vmem(),
        cost_estimate=pl.CostEstimate(flops=1000000, bytes_accessed=100000, transcendentals=0),
        grid=(1,),
compiler_params=pltpu.CompilerParams(vmem_limit_bytes=GRANT),
        name="apply",
    )(lost, gas_at, core, energy)


def spread_kernel(group, coord_ref, vel_ref, mass_ref, soft_ref, pairs_ref, count_ref, out_ref, pairs_out, count_out):
    pairs_out[...] = pairs_ref[...]
    count_out[...] = count_ref[...]
    lines = [coord_ref[f] for f in range(3)] + [vel_ref[f] for f in range(3)] + [mass_ref[0], soft_ref[0]]
    out_ref[...] = jnp.broadcast_to(jnp.concatenate(lines, axis=0)[None], (group, 8, LANES))


def spread(coord, vel, mass, soft, pairs, count, group):
    return pl.pallas_call(
        functools.partial(spread_kernel, group),
        out_shape=(
            jax.ShapeDtypeStruct((group, 8, LANES), jnp.float32),
            jax.ShapeDtypeStruct((2, NPAIR), jnp.int32),
            jax.ShapeDtypeStruct((1, LANES), jnp.int32),
        ),
        in_specs=[vmem()] * 6,
        out_specs=(vmem(),) * 3,
        compiler_params=pltpu.CompilerParams(vmem_limit_bytes=GRANT),
        name="spread",
    )(coord, vel, mass, soft, pairs, count)


def settle_kernel(group, arrived_ref, out_ref):
    lane = lax.broadcasted_iota(jnp.int32, (group, LANES), 1).astype(jnp.float32)
    parts = [jnp.broadcast_to(arrived_ref[:, f : f + 1], (group, LANES)) for f in range(6)]
    at_first = lane == parts[0]
    at_second = lane == parts[3]
    for k in range(2):
        value = jnp.where(at_first, parts[1 + k], jnp.where(at_second, parts[4 + k], 0.0))
        out_ref[k] = jnp.sum(value, axis=0, keepdims=True)


def settle(arrived, group):
    return pl.pallas_call(
        functools.partial(settle_kernel, group),
        out_shape=jax.ShapeDtypeStruct((2, 1, LANES), jnp.float32),
        in_specs=[vmem()],
        out_specs=vmem(),
compiler_params=pltpu.CompilerParams(vmem_limit_bytes=GRANT),
        name="settle",
    )(arrived)


def body(gas_core, gas_vel, gas_energy, cell_pairs, bh_coord, bh_vel, bh_mass, bh_soft, mem_gas, mem_slot, send_count):
    group = lax.axis_size("dy") * lax.axis_size("dz")
    deep = lax.axis_size("dz")
    z_length = cell_height * CPD * deep
    y_length = face_width * lax.axis_size("dy")
    core = gas_core.reshape(5, ROWS, LANES)
    energy = gas_energy.reshape(ROWS, LANES)
    ranked, back, tail, head = order(core)
    lower = lax.ppermute(tail, "dz", [(i, (i + 1) % deep) for i in range(deep)])
    upper = lax.ppermute(head, "dz", [((i + 1) % deep, i) for i in range(deep)])
    copies, pairs, count = spread(
        bh_coord.reshape(3, 1, LANES),
        bh_vel.reshape(3, 1, LANES),
        bh_mass.reshape(1, 1, LANES),
        bh_soft.reshape(1, 1, LANES),
        cell_pairs.reshape(2, NPAIR),
        send_count.reshape(1, LANES),
        group,
    )
    holes = lax.all_to_all(copies, ("dy", "dz"), split_axis=0, concat_axis=0, tiled=True).reshape(group * 8, LANES)
    own = own_density(ranked, z_length)
    rho, picked, place = pairs_density(
        pairs,
        ranked,
        lower,
        upper,
        own,
        back,
        core,
        gas_vel.reshape(3, ROWS, LANES),
        energy.reshape(1, ROWS, LANES),
        mem_gas.reshape(CAP, LANES),
        mem_slot.reshape(CAP, LANES),
        z_length,
    )
    message, lost, gas_at = feed(picked, place, count, holes, y_length, z_length, group)
    arrived = lax.all_to_all(message, ("dy", "dz"), split_axis=0, concat_axis=0, tiled=True)
    update = apply(lost, gas_at, core, energy)
    bh_update = settle(arrived, group)
    return (
        rho.reshape(1, 1, CPD * CELL),
        update.reshape(2, 1, 1, CPD * CELL),
        bh_update.reshape(2, 1, 1, LANES),
    )


def solution(mesh):
    lead, plain = P(None, "dx", "dy", "dz"), P("dx", "dy", "dz")
    in_specs = (lead, lead, plain, lead, lead, lead, plain, plain, plain, plain, plain)
    return jax.shard_map(body, mesh=mesh, in_specs=in_specs, out_specs=(plain, lead, lead), check_vma=False)
```
